256 devices in a mesh: inst: 8 (over x, y_lo), space: 32 (over z, y_hi, core).
Axes of the slice: x: 4, y: 4 (y_hi: 2, y_lo: 2; y = y_hi * 2 + y_lo), z: 8, core: 2. Of those that a mesh axis runs over, the one named last changes fastest.
Arguments:
- adjoint: float32 [8, 5, 256, 64, 128], P('inst', None, 'space'), may hold values from -6 to 6
- source: float32 [8, 5, 256, 64, 128], P('inst', None, 'space'), may hold values from -6 to 6
- viscosity: float32 [256, 64, 128], P('space'), may hold values from 0.2 to 2
- kappa: float32 [5], replicated, may hold values from 0.5 to 2
- coupling: float32 [5, 5], replicated, may hold values from -2.4 to 2.4
- bc_flags: int32 [5, 3], replicated, may hold values 0 or 1
- inst_map: int32 [8], replicated, may hold values from 0 to 7, each once
Outputs:
- residual: float32 [8, 5, 256, 64, 128], P('inst', None, 'space')
The draws below stay inside these ranges and needn't reach their ends.
Inputs may be any that keep to these rules, and one draw needn't show every extreme that they name: `inst_map`: a permutation of 0 to 7. `bc_flags`: 1 marks a face of zero normal flux, 0 a face held at zero.
All inputs are finite; a program needn't handle non-finite values.
Results may differ from the reference program's by a relative error of at most 0.0001.
Values sent between devices are 32-bit elements; how exact they have to be, the bound alone decides.
A program may use at most 128 MiB of HBM per device.

```python
import math
import jax
import jax.numpy as jnp
from jax import lax

NTH = 256
NR = 64
NX = 128
N_INST = 8


def plant(values, own_key, smallest, high):
    dims = values.shape
    place = [jax.random.randint(jax.random.fold_in(own_key, axis), (), 0, dims[axis]) for axis in range(len(dims))]
    values = values.at[tuple(place)].set(smallest)
    longest = dims.index(max(dims))
    place[longest] = (place[longest] + 1) % dims[longest]
    return values.at[tuple(place)].set(high)


def steps_of(stream_key, dims, pieces, low, largest):
    factor_of, own = 1.0, jax.random.fold_in(stream_key, 6)
    for dim, blocks in pieces:
        steps = jnp.exp(jax.random.uniform(jax.random.fold_in(own, dim), (blocks,), jnp.float32, low / len(pieces), largest / len(pieces)))
        factor_of = factor_of * jnp.repeat(steps, dims[dim] // blocks).reshape([-1 if axis == dim else 1 for axis in range(len(dims))])
    return factor_of


def scatter_about(own_key, shape, width, most, split=(), kind=jnp.bfloat16):
    result = jax.random.normal(own_key, shape, jnp.float32) * width
    if len(split) > 0:
        result = steps_of(own_key, shape, split, -0.22, 0.18) * result
    return jnp.clip(result, min=-most, max=most).astype(kind)


def setup_inputs(seed: int = 0) -> dict:
    key_list = jax.random.split(jax.random.key(seed), 8)
    return {
        "adjoint": scatter_about(key_list[0], (N_INST, 5, NTH, NR, NX), 1.0, 6.0, ((0, 8), (2, 32)), jnp.float32),
        "source": scatter_about(key_list[1], (N_INST, 5, NTH, NR, NX), 1.0, 6.0, ((0, 8), (2, 32)), jnp.float32),
        "viscosity": jnp.clip(jnp.exp(math.log(2.0) - 2.3025851 * jax.random.uniform(key_list[2], (NTH, NR, NX), jnp.float32) ** steps_of(key_list[2], (NTH, NR, NX), ((0, 32),), -0.2, 0.2)), 0.2, 2.0),
        "kappa": jnp.clip(jnp.exp(jax.random.uniform(key_list[3], (5,), jnp.float32, math.log(0.5), math.log(2.0))), 0.5, 2.0),
        "coupling": scatter_about(key_list[4], (5, 5), 0.4, 2.4, (), jnp.float32),
        "bc_flags": plant((jax.random.randint(key_list[5], (5, 3), 0, 2) < 1).astype(jnp.int32), jax.random.fold_in(key_list[5], 1), 0, 1),
        "inst_map": jax.random.permutation(key_list[6], N_INST).astype(jnp.int32),
    }


def spectral_matrix(labels, slots):
    labels = labels.astype(jnp.int32)
    offset = labels[:, None] - labels[None, :]
    parity = (1 - 2 * (jnp.abs(offset) % 2)).astype(jnp.float32)
    sines = jnp.sin(jnp.pi * offset.astype(jnp.float32) / slots)
    safe = jnp.where(offset == 0, jnp.float32(1.0), sines)
    return jnp.where(offset == 0, jnp.float32(0.0), 0.5 * parity / safe)


def mode_tables(points):
    indices = jnp.arange(points, dtype=jnp.int32)
    product = (indices[:, None] * indices[None, :]) % points
    angles = 2.0 * jnp.pi * product.astype(jnp.float32) / points
    return jnp.cos(angles), jnp.sin(angles)


def cycle_response(points, cycle_index, near):
    indices = jnp.arange(points, dtype=jnp.int32)
    wave_number = jnp.minimum(indices, points - indices)
    cutoff = jnp.maximum(4, (points * (cycle_index + 1)) // (2 * near))
    return (wave_number[None, :] < cutoff[:, None]).astype(jnp.float32)


def smooth_cycles(pencil, first_cycle, near):
    points = pencil.shape[1]
    cycles = pencil.shape[2]
    cosines, sines_table = mode_tables(points)
    cycle_index = first_cycle + jnp.arange(cycles, dtype=jnp.int32)
    response = (cycle_response(points, cycle_index, near).T / points)[None, :, :, None]
    coef_cos = jnp.einsum("tk,ftrx->fkrx", cosines, pencil, precision=lax.Precision.HIGHEST)
    coef_sin = jnp.einsum("tk,ftrx->fkrx", sines_table, pencil, precision=lax.Precision.HIGHEST)
    smoothed = jnp.einsum("tk,fkrx->ftrx", cosines, coef_cos * response, precision=lax.Precision.HIGHEST)
    smoothed = smoothed + jnp.einsum("tk,fkrx->ftrx", sines_table, coef_sin * response, precision=lax.Precision.HIGHEST)
    weights = jnp.maximum(1.0 - cycle_index.astype(jnp.float32) / near, 0.0)[None, None, :, None]
    return pencil + weights * (smoothed - pencil)


def viscous(center, nbr_up, nbr_dn, visc, visc_up, visc_dn, kappa, flags):
    cycles = center.shape[2]
    cells_x = center.shape[3]
    cycle_weight = (1.0 / (jnp.arange(cycles, dtype=jnp.float32) + 1.0))[None, :, None]
    theta = cycle_weight * (0.5 * (visc + visc_up) * (center - nbr_up) + 0.5 * (visc + visc_dn) * (center - nbr_dn))
    face_r = 0.5 * (visc[:, :-1, :] + visc[:, 1:, :])
    flux_r = face_r * (center[:, :, :-1, :] - center[:, :, 1:, :])
    radial = jnp.pad(flux_r, ((0, 0), (0, 0), (0, 1), (0, 0))) - jnp.pad(flux_r, ((0, 0), (0, 0), (1, 0), (0, 0)))
    face_x = 0.5 * (visc[:, :, :-1] + visc[:, :, 1:])
    flux_x = face_x * (center[:, :, :, :-1] - center[:, :, :, 1:])
    axial = jnp.pad(flux_x, ((0, 0), (0, 0), (0, 0), (0, 1))) - jnp.pad(flux_x, ((0, 0), (0, 0), (0, 0), (1, 0)))
    open_faces = (1 - flags).astype(jnp.float32)
    outer = open_faces[:, 2][:, None, None, None] * visc[None, :, -1:, :] * center[:, :, -1:, :]
    outer = jnp.pad(outer, ((0, 0), (0, 0), (cycles - 1, 0), (0, 0)))
    inflow = open_faces[:, 0][:, None, None, None] * visc[None, :, :, :1] * center[:, :, :, :1]
    inflow = jnp.pad(inflow, ((0, 0), (0, 0), (0, 0), (0, cells_x - 1)))
    outflow = open_faces[:, 1][:, None, None, None] * visc[None, :, :, -1:] * center[:, :, :, -1:]
    outflow = jnp.pad(outflow, ((0, 0), (0, 0), (0, 0), (cells_x - 1, 0)))
    return kappa[:, None, None, None] * (theta + radial + axial + outer + inflow + outflow)


def reference(adjoint, source, viscosity, kappa, coupling, bc_flags, inst_map):
    matrix = spectral_matrix(inst_map, N_INST)
    near = NR // 2
    visc_up = jnp.roll(viscosity, -1, axis=0)
    visc_dn = jnp.roll(viscosity, 1, axis=0)
    results = []
    for slot in range(N_INST):
        center = adjoint[slot]
        spectral = jnp.tensordot(matrix[:, slot], adjoint, axes=1, precision=lax.Precision.HIGHEST)
        coupled = jnp.einsum("gf,gtrx->ftrx", coupling, center, precision=lax.Precision.HIGHEST)
        diffused = viscous(center, jnp.roll(center, -1, axis=1), jnp.roll(center, 1, axis=1), viscosity, visc_up, visc_dn, kappa, bc_flags)
        pre = source[slot] + coupled + diffused + spectral
        inner = smooth_cycles(pre[:, :, :near, :], jnp.int32(0), near)
        results.append(jnp.concatenate([inner, pre[:, :, near:, :]], axis=2))
    return jnp.stack(results, axis=0)
```

```python
import functools

import jax
import jax.numpy as jnp
import numpy as np
from jax import lax
from jax.experimental import pallas as pl
from jax.experimental.pallas import tpu as pltpu
from jax.sharding import PartitionSpec as P

FIELDS, SECTOR, CYCLES, CELLS_X = 5, 8, 64, 128
POINTS, NEAR, SLOTS, SECTORS = 256, 32, 8, 32
GROUPS = ((0, 2), (2, 5))
MESH = pl.DeviceIdType.MESH


def slot_table():
    offset = np.arange(-(SLOTS - 1), SLOTS + 1)
    parity = 1.0 - 2.0 * (np.abs(offset) % 2)
    sines = np.sin(np.pi * offset / SLOTS)
    inner = (offset != 0) & (np.abs(offset) < SLOTS)
    table = np.where(inner, 0.5 * parity / np.where(inner, sines, 1.0), 0.0)
    return jnp.asarray(table.astype(np.float32))


def kernel(adj, src, visc, kap, cpl, bcf, imap, tab, out, *scratch):
    count = len(GROUPS)
    names = iter(scratch)
    take = lambda n: [next(names) for _ in range(n)]
    adjx, mux, local, outv, mtab = take(5)
    recv_a = take(count + 1)
    mixed = take(count + 1)
    spec = take(count + 1)
    stage_e, recv_e, stage_g, recv_g = take(count), take(count), take(count), take(count)
    load_sem, halo_send, halo_recv, own_sem, out_sem = take(5)
    a_send, a_recv, c_send, c_recv = take(4)
    e_send, e_recv, g_send, g_recv = take(4)

    me, sp = lax.axis_index("inst"), lax.axis_index("space")
    ix, iy = lax.div(me, 2), lax.rem(me, 2)
    sz, sy, sc = lax.div(sp, 4), lax.rem(lax.div(sp, 2), 2), lax.rem(sp, 2)

    def inst_at(k, sign):
        kx, ky = k // 2, k % 2
        return lax.rem(ix + sign * kx + 4, 4) * 2 + lax.rem(iy + ky, 2)

    def space_at(i, sign):
        step = lax.div(i, 4)
        kz = lax.div(step + 1, 2) * (1 - 2 * lax.rem(step, 2))
        return (
            lax.rem(sz + sign * kz + 8, 8) * 4
            + lax.rem(sy + lax.rem(lax.div(i, 2), 2), 2) * 2
            + lax.rem(sc + lax.rem(i, 2), 2)
        )

    loads = [
        pltpu.make_async_copy(visc, mux.at[pl.ds(1, SECTOR)], load_sem.at[0]),
        pltpu.make_async_copy(adj.at[0], adjx.at[:, pl.ds(1, SECTOR)], load_sem.at[1]),
        pltpu.make_async_copy(src.at[0], local, load_sem.at[2]),
    ]
    bounds = [(lo, hi, 0) for lo, hi in GROUPS] + [(0, FIELDS, NEAR)]

    def chunk(g, slot):
        lo, hi, first = bounds[g]
        return adj.at[0, pl.ds(lo, hi - lo), slot, pl.ds(first, NEAR), :]

    own_a = [
        pltpu.make_async_copy(chunk(g, me), recv_a[g].at[me], own_sem.at[0, g])
        for g in range(count + 1)
    ]
    own_c = [
        pltpu.make_async_copy(mixed[g].at[me], spec[g].at[:, me], own_sem.at[1, g])
        for g in range(count + 1)
    ]

    def rows(g, index):
        depth = (bounds[g][1] - bounds[g][0]) * SECTOR
        return pl.ds(pl.multiple_of(index * depth, 8), depth)

    own_e = [
        pltpu.make_async_copy(
            stage_e[g].at[rows(g, sp)], recv_e[g].at[rows(g, sp)], own_sem.at[2, g]
        )
        for g in range(count)
    ]
    own_g = [
        pltpu.make_async_copy(
            stage_g[g].at[rows(g, sp)], recv_g[g].at[rows(g, sp)], own_sem.at[3, g]
        )
        for g in range(count)
    ]

    def send_a(g, k):
        return pltpu.make_async_remote_copy(
            src_ref=chunk(g, inst_at(k, 1)),
            dst_ref=recv_a[g].at[me],
            send_sem=a_send.at[g, k],
            recv_sem=a_recv.at[g, k],
            device_id={"inst": inst_at(k, 1)},
            device_id_type=MESH,
        )

    def arrive_a(g, k):
        return pltpu.make_async_remote_copy(
            src_ref=chunk(g, me),
            dst_ref=recv_a[g].at[inst_at(k, -1)],
            send_sem=a_send.at[g, k],
            recv_sem=a_recv.at[g, k],
            device_id={"inst": inst_at(k, 1)},
            device_id_type=MESH,
        )

    def send_c(g, k):
        return pltpu.make_async_remote_copy(
            src_ref=mixed[g].at[inst_at(k, 1)],
            dst_ref=spec[g].at[:, me],
            send_sem=c_send.at[g, k],
            recv_sem=c_recv.at[g, k],
            device_id={"inst": inst_at(k, 1)},
            device_id_type=MESH,
        )

    def arrive_c(g, k):
        return pltpu.make_async_remote_copy(
            src_ref=mixed[g].at[me],
            dst_ref=spec[g].at[:, inst_at(k, -1)],
            send_sem=c_send.at[g, k],
            recv_sem=c_recv.at[g, k],
            device_id={"inst": inst_at(k, 1)},
            device_id_type=MESH,
        )

    def send_s(stage, recv, send_sem, recv_sem, g, i, slot):
        return pltpu.make_async_remote_copy(
            src_ref=stage[g].at[rows(g, space_at(i, 1))],
            dst_ref=recv[g].at[rows(g, slot)],
            send_sem=send_sem.at[g, i],
            recv_sem=recv_sem.at[g, i],
            device_id={"space": space_at(i, 1)},
            device_id_type=MESH,
        )

    after, before = lax.rem(sp + 1, SECTORS), lax.rem(sp + SECTORS - 1, SECTORS)

    def halo(index, source, target, peer):
        return pltpu.make_async_remote_copy(
            src_ref=source,
            dst_ref=target,
            send_sem=halo_send.at[index],
            recv_sem=halo_recv.at[index],
            device_id={"space": peer},
            device_id_type=MESH,
        )

    halos = [
        halo(0, adj.at[0, :, SECTOR - 1], adjx.at[:, 0], after),
        halo(1, adj.at[0, :, 0], adjx.at[:, SECTOR + 1], before),
        halo(2, visc.at[SECTOR - 1], mux.at[0], after),
        halo(3, visc.at[0], mux.at[SECTOR + 1], before),
    ]

    barrier = pltpu.get_barrier_semaphore()
    for k in range(1, SLOTS):
        pl.semaphore_signal(
            barrier, inc=1, device_id={"inst": inst_at(k, 1)}, device_id_type=MESH
        )

    @pl.loop(1, SECTORS)
    def _(i):
        pl.semaphore_signal(
            barrier, inc=1, device_id={"space": space_at(i, 1)}, device_id_type=MESH
        )

    for copy in loads:
        copy.start()
    for copy in own_a:
        copy.start()
    pl.semaphore_wait(barrier, SLOTS - 1 + SECTORS - 1)

    for g in range(count):
        for k in range(1, SLOTS):
            send_a(g, k).start()
        if g == 0:
            for copy in halos:
                copy.start()

    cutoff = jnp.maximum(4, lax.div(POINTS * (sp + 1), 2 * NEAR))
    width = 2 * cutoff - 1
    weight = 1.0 - sp.astype(jnp.float32) / NEAR

    @pl.loop(0, POINTS // 32)
    def _(b):
        row = lax.broadcasted_iota(jnp.int32, (32, POINTS), 0) + b * 32
        col = lax.broadcasted_iota(jnp.int32, (32, POINTS), 1)
        gap = (row - col + POINTS) & (POINTS - 1)
        top = jnp.sin(((gap * width) & (2 * POINTS - 1)).astype(jnp.float32) * (np.pi / POINTS))
        low = jnp.sin(gap.astype(jnp.float32) * (np.pi / POINTS))
        same = gap == 0
        ratio = top / jnp.where(same, 1.0, low)
        table = jnp.where(same, width.astype(jnp.float32), ratio) * (1.0 / POINTS)
        mtab[pl.ds(pl.multiple_of(b * 32, 32), 32), :] = weight * table + jnp.where(
            same, 1.0 - weight, 0.0
        )

    def mix(g):
        own_a[g].wait()
        for k in range(1, SLOTS):
            arrive_a(g, k).wait_recv()
        fields = bounds[g][1] - bounds[g][0]
        coef = {
            (j, n): tab[imap[j] - imap[n] + SLOTS - 1]
            for n in range(SLOTS)
            for j in range(n + 1, SLOTS)
        }

        @pl.loop(0, fields * NEAR // 8)
        def _(b):
            fi, r0 = lax.div(b, NEAR // 8), lax.rem(b, NEAR // 8) * 8
            block = pl.ds(pl.multiple_of(r0, 8), 8)
            values = [recv_a[g][j, fi, block, :] for j in range(SLOTS)]
            for n in range(SLOTS):
                total = None
                for j in range(SLOTS):
                    if j == n:
                        continue
                    term = coef[max(j, n), min(j, n)] * values[j]
                    if total is None:
                        total = term if j > n else -term
                    else:
                        total = total + term if j > n else total - term
                mixed[g][n, fi, block, :] = total

        for k in range(1, SLOTS):
            send_c(g, k).start()
        own_c[g].start()

    for g in range(count):
        mix(g)
    for k in range(1, SLOTS):
        send_a(count, k).start()

    for copy in loads:
        copy.wait()
    for copy in halos:
        copy.wait_recv()

    row = lax.broadcasted_iota(jnp.int32, (CYCLES, CELLS_X), 0)
    col = lax.broadcasted_iota(jnp.int32, (CYCLES, CELLS_X), 1)

    @pl.loop(0, SECTOR)
    def _(t):
        mu = mux[t + 1]
        half_cycle = 0.5 / (row.astype(jnp.float32) + 1.0)
        up = half_cycle * (mu + mux[t + 2])
        down = half_cycle * (mu + mux[t])
        out_r = jnp.where(
            row < CYCLES - 1, 0.5 * (mu + pltpu.roll(mu, CYCLES - 1, 0)), 0.0
        )
        in_r = pltpu.roll(out_r, 1, 0)
        out_x = jnp.where(
            col < CELLS_X - 1, 0.5 * (mu + pltpu.roll(mu, CELLS_X - 1, 1)), 0.0
        )
        in_x = pltpu.roll(out_x, 1, 1)
        own = up + down + out_r + in_r + out_x + in_x
        for f in range(FIELDS):
            p = adjx[f, t + 1]
            face = [1.0 - bcf[f, i].astype(jnp.float32) for i in range(3)]
            edge = (
                jnp.where(row == CYCLES - 1, face[2], 0.0)
                + jnp.where(col == 0, face[0], 0.0)
                + jnp.where(col == CELLS_X - 1, face[1], 0.0)
            )
            diffused = (own + edge * mu) * p
            diffused = diffused - up * adjx[f, t + 2] - down * adjx[f, t]
            diffused = diffused - out_r * pltpu.roll(p, CYCLES - 1, 0)
            diffused = diffused - in_r * pltpu.roll(p, 1, 0)
            diffused = diffused - out_x * pltpu.roll(p, CELLS_X - 1, 1)
            diffused = diffused - in_x * pltpu.roll(p, 1, 1)
            total = local[f, t] + kap[f] * diffused
            for g in range(FIELDS):
                total = total + cpl[g, f] * adjx[g, t + 1]
            local[f, t] = total

    for g in range(count):
        lo, hi, _ = bounds[g]
        own_c[g].wait()
        for k in range(1, SLOTS):
            arrive_c(g, k).wait_recv()
        stride = (hi - lo) * SECTOR

        @pl.loop(0, SECTOR)
        def _(t):
            for f in range(lo, hi):
                for b in range(NEAR // 8):
                    block = pl.ds(b * 8, 8)
                    value = local[f, t, block, :] + spec[g][f - lo, t, block, :]
                    start = b * 8 * stride + (f - lo) * SECTOR + t
                    stage_e[g][pl.ds(start, 8, stride=stride), :] = value

        own_e[g].start()

        @pl.loop(1, SECTORS)
        def _(i):
            send_s(stage_e, recv_e, e_send, e_recv, g, SECTORS - i, sp).start()

    mix(count)

    for g in range(count):
        lo, hi, _ = bounds[g]
        own_e[g].wait()

        @pl.loop(1, SECTORS)
        def _(i):
            send_s(
                stage_e, recv_e, e_send, e_recv, g, SECTORS - i, space_at(SECTORS - i, -1)
            ).wait_recv()

        pencils = recv_e[g][...].reshape(SECTORS, (hi - lo) * SECTOR, CELLS_X)
        parts = []
        for f in range(hi - lo):
            pencil = pencils[:, f * SECTOR : (f + 1) * SECTOR, :].reshape(POINTS, CELLS_X)
            smooth = jnp.dot(
                mtab[...],
                pencil,
                precision=lax.Precision.HIGHEST,
                preferred_element_type=jnp.float32,
            )
            parts.append(smooth.reshape(SECTORS, SECTOR, CELLS_X))
        stage_g[g][...] = jnp.concatenate(parts, axis=1).reshape(
            SECTORS * (hi - lo) * SECTOR, CELLS_X
        )
        own_g[g].start()

        @pl.loop(1, SECTORS)
        def _(i):
            send_s(stage_g, recv_g, g_send, g_recv, g, SECTORS - i, sp).start()

    own_c[count].wait()
    for k in range(1, SLOTS):
        arrive_c(count, k).wait_recv()

    @pl.loop(0, SECTOR)
    def _(t):
        for f in range(FIELDS):
            outv[f, t, pl.ds(NEAR, NEAR), :] = (
                local[f, t, pl.ds(NEAR, NEAR), :] + spec[count][f, t]
            )

    far = pltpu.make_async_copy(
        outv.at[:, :, pl.ds(NEAR, NEAR), :],
        out.at[0, :, :, pl.ds(NEAR, NEAR), :],
        out_sem.at[count],
    )
    far.start()
    writes = [far]

    for g in range(count):
        lo, hi, _ = bounds[g]
        own_g[g].wait()

        @pl.loop(1, SECTORS)
        def _(i):
            send_s(
                stage_g, recv_g, g_send, g_recv, g, SECTORS - i, space_at(SECTORS - i, -1)
            ).wait_recv()

        stride = (hi - lo) * SECTOR

        @pl.loop(0, SECTOR)
        def _(t):
            for f in range(lo, hi):
                for b in range(NEAR // 8):
                    start = b * 8 * stride + (f - lo) * SECTOR + t
                    outv[f, t, pl.ds(b * 8, 8), :] = recv_g[g][
                        pl.ds(start, 8, stride=stride), :
                    ]

        write = pltpu.make_async_copy(
            outv.at[pl.ds(lo, hi - lo), :, pl.ds(0, NEAR), :],
            out.at[0, pl.ds(lo, hi - lo), :, pl.ds(0, NEAR), :],
            out_sem.at[g],
        )
        write.start()
        writes.append(write)

    for copy in halos:
        copy.wait_send()
    for g in range(count + 1):
        for k in range(1, SLOTS):
            send_a(g, k).wait_send()
            send_c(g, k).wait_send()
    for g in range(count):

        @pl.loop(1, SECTORS)
        def _(i):
            send_s(stage_e, recv_e, e_send, e_recv, g, SECTORS - i, sp).wait_send()
            send_s(stage_g, recv_g, g_send, g_recv, g, SECTORS - i, sp).wait_send()

    for copy in writes:
        copy.wait()


def body(adjoint, source, viscosity, kappa, coupling, bc_flags, inst_map):
    count = len(GROUPS)
    sizes = [hi - lo for lo, hi in GROUPS]
    f32 = jnp.float32
    vmem, dma = pltpu.VMEM, pltpu.SemaphoreType.DMA
    slabs = [vmem((SLOTS, n, NEAR, CELLS_X), f32) for n in sizes + [FIELDS]]
    sectors = [vmem((n, SECTOR, NEAR, CELLS_X), f32) for n in sizes + [FIELDS]]
    pencils = [vmem((SECTORS * n * SECTOR, CELLS_X), f32) for n in sizes]
    scratch = [
        vmem((FIELDS, SECTOR + 2, CYCLES, CELLS_X), f32),
        vmem((SECTOR + 2, CYCLES, CELLS_X), f32),
        vmem((FIELDS, SECTOR, CYCLES, CELLS_X), f32),
        vmem((FIELDS, SECTOR, CYCLES, CELLS_X), f32),
        vmem((POINTS, POINTS), f32),
        *slabs,
        *slabs,
        *sectors,
        *(pencils * 4),
        dma((3,)),
        dma((4,)),
        dma((4,)),
        dma((4, count + 1)),
        dma((count + 1,)),
        *[dma((count + 1, SLOTS))] * 4,
        *[dma((count, SECTORS))] * 4,
    ]
    hbm, smem = pl.BlockSpec(memory_space=pl.ANY), pl.BlockSpec(memory_space=pltpu.SMEM)
    return pl.pallas_call(
        kernel,
        out_shape=jax.ShapeDtypeStruct(adjoint.shape, f32),
        in_specs=[hbm] * 3 + [smem] * 5,
        out_specs=hbm,
        scratch_shapes=scratch,
        compiler_params=pltpu.CompilerParams(
            collective_id=0, has_side_effects=True, vmem_limit_bytes=48 * 1024 * 1024
        ),
        name="residual",
    )(adjoint, source, viscosity, kappa, coupling, bc_flags, inst_map, slot_table())


def solution(mesh):
    return jax.shard_map(
        body,
        mesh=mesh,
        in_specs=(
            P("inst", None, "space", None, None),
            P("inst", None, "space", None, None),
            P("space", None, None),
            P(),
            P(),
            P(),
            P(),
        ),
        out_specs=P("inst", None, "space", None, None),
        check_vma=False,
    )
```

```python
import functools

import jax
import jax.numpy as jnp
import numpy as np
from jax import lax
from jax.experimental import pallas as pl
from jax.experimental.pallas import tpu as pltpu
from jax.sharding import PartitionSpec as P

FIELDS, SECTOR, CYCLES, CELLS_X = 5, 8, 64, 128
POINTS, NEAR, SLOTS, SECTORS = 256, 32, 8, 32
GROUPS = ((0, 2), (2, 5))
MESH = pl.DeviceIdType.MESH


def slot_table():
    offset = np.arange(-(SLOTS - 1), SLOTS + 1)
    parity = 1.0 - 2.0 * (np.abs(offset) % 2)
    sines = np.sin(np.pi * offset / SLOTS)
    inner = (offset != 0) & (np.abs(offset) < SLOTS)
    table = np.where(inner, 0.5 * parity / np.where(inner, sines, 1.0), 0.0)
    return jnp.asarray(table.astype(np.float32))


def kernel(adj, src, visc, *refs):
    smalls, out, scratch = refs[:5], refs[5], refs[6:]
    count = len(GROUPS)
    names = iter(scratch)
    take = lambda n: [next(names) for _ in range(n)]
    adjx, mux, local, mtab = take(4)
    recv_a = take(count + 1)
    mixed = take(count + 1)
    spec = take(count + 1)
    stage_e, recv_e, stage_g, recv_g = take(count), take(count), take(count), take(count)
    load_sem, halo_send, halo_recv, own_sem = take(4)
    held = take(5)
    kap, cpl, bcf, imap, tab = held
    a_send, a_recv, c_send, c_recv = take(4)
    e_send, e_recv, g_send, g_recv = take(4)

    me, sp = lax.axis_index("inst"), lax.axis_index("space")
    ix, iy = lax.div(me, 2), lax.rem(me, 2)
    sz, sy, sc = lax.div(sp, 4), lax.rem(lax.div(sp, 2), 2), lax.rem(sp, 2)

    flip_y = [iy, lax.rem(iy + 1, 2)]
    turn_x = [lax.rem(ix + k, 4) * 2 for k in range(4)]
    turn_z = [lax.rem(sz + k, 8) * 4 for k in range(8)]
    flip_s = [sy * 2, lax.rem(sy + 1, 2) * 2]
    flip_c = [sc, lax.rem(sc + 1, 2)]

    def inst_at(k, sign):
        return turn_x[(sign * (k // 2)) % 4] + flip_y[k % 2]

    def space_at(i, sign):
        step = i // 4
        kz = (step + 1) // 2 * (1 - 2 * (step % 2))
        return turn_z[(sign * kz) % 8] + flip_s[i // 2 % 2] + flip_c[i % 2]

    loads = [
        pltpu.make_async_copy(visc, mux.at[pl.ds(1, SECTOR)], load_sem.at[0]),
        pltpu.make_async_copy(adj.at[0], adjx.at[:, pl.ds(1, SECTOR)], load_sem.at[1]),
        pltpu.make_async_copy(src.at[0], local, load_sem.at[2]),
    ]
    consts = [
        pltpu.make_async_copy(small, ref, load_sem.at[3 + i])
        for i, (small, ref) in enumerate(zip(smalls, held))
    ]
    bounds = [(lo, hi, 0) for lo, hi in GROUPS] + [(0, FIELDS, NEAR)]

    def chunk(g, slot):
        lo, hi, first = bounds[g]
        return adj.at[0, pl.ds(lo, hi - lo), slot, pl.ds(first, NEAR), :]

    own_a = [
        pltpu.make_async_copy(chunk(g, me), recv_a[g].at[me], own_sem.at[0, g])
        for g in range(count + 1)
    ]
    own_c = [
        pltpu.make_async_copy(mixed[g].at[me], spec[g].at[:, me], own_sem.at[1, g])
        for g in range(count + 1)
    ]

    def rows(g, index):
        depth = (bounds[g][1] - bounds[g][0]) * SECTOR
        return pl.ds(pl.multiple_of(index * depth, 8), depth)

    own_e = [
        pltpu.make_async_copy(
            stage_e[g].at[rows(g, sp)], recv_e[g].at[rows(g, sp)], own_sem.at[2, g]
        )
        for g in range(count)
    ]
    own_g = [
        pltpu.make_async_copy(
            stage_g[g].at[rows(g, sp)], recv_g[g].at[rows(g, sp)], own_sem.at[3, g]
        )
        for g in range(count)
    ]

    def send_a(g, k):
        return pltpu.make_async_remote_copy(
            src_ref=chunk(g, inst_at(k, 1)),
            dst_ref=recv_a[g].at[me],
            send_sem=a_send.at[g, k],
            recv_sem=a_recv.at[g, k],
            device_id={"inst": inst_at(k, 1)},
            device_id_type=MESH,
        )

    def arrive_a(g, k):
        return pltpu.make_async_remote_copy(
            src_ref=chunk(g, me),
            dst_ref=recv_a[g].at[inst_at(k, -1)],
            send_sem=a_send.at[g, k],
            recv_sem=a_recv.at[g, k],
            device_id={"inst": inst_at(k, 1)},
            device_id_type=MESH,
        )

    def send_c(g, k):
        return pltpu.make_async_remote_copy(
            src_ref=mixed[g].at[inst_at(k, 1)],
            dst_ref=spec[g].at[:, me],
            send_sem=c_send.at[g, k],
            recv_sem=c_recv.at[g, k],
            device_id={"inst": inst_at(k, 1)},
            device_id_type=MESH,
        )

    def arrive_c(g, k):
        return pltpu.make_async_remote_copy(
            src_ref=mixed[g].at[me],
            dst_ref=spec[g].at[:, inst_at(k, -1)],
            send_sem=c_send.at[g, k],
            recv_sem=c_recv.at[g, k],
            device_id={"inst": inst_at(k, 1)},
            device_id_type=MESH,
        )

    def send_s(stage, recv, send_sem, recv_sem, g, i, slot):
        return pltpu.make_async_remote_copy(
            src_ref=stage[g].at[rows(g, space_at(i, 1))],
            dst_ref=recv[g].at[rows(g, slot)],
            send_sem=send_sem.at[g, i],
            recv_sem=recv_sem.at[g, i],
            device_id={"space": space_at(i, 1)},
            device_id_type=MESH,
        )

    after, before = lax.rem(sp + 1, SECTORS), lax.rem(sp + SECTORS - 1, SECTORS)

    def halo(index, source, target, peer):
        return pltpu.make_async_remote_copy(
            src_ref=source,
            dst_ref=target,
            send_sem=halo_send.at[index],
            recv_sem=halo_recv.at[index],
            device_id={"space": peer},
            device_id_type=MESH,
        )

    def halos_of(part):
        span = pl.ds(part * NEAR, NEAR)
        first, last = SECTOR - 1, SECTOR + 1
        return [
            halo(4 * part, adj.at[0, :, first, span], adjx.at[:, 0, span], after),
            halo(4 * part + 1, adj.at[0, :, 0, span], adjx.at[:, last, span], before),
            halo(4 * part + 2, visc.at[first, span], mux.at[0, span], after),
            halo(4 * part + 3, visc.at[0, span], mux.at[last, span], before),
        ]

    halos = [halos_of(0), halos_of(1)]

    barrier = pltpu.get_barrier_semaphore()
    for k in range(1, SLOTS):
        pl.semaphore_signal(
            barrier, inc=1, device_id={"inst": inst_at(k, 1)}, device_id_type=MESH
        )

    for i in range(SECTORS - 1, 0, -1):
        pl.semaphore_signal(
            barrier, inc=1, device_id={"space": space_at(i, 1)}, device_id_type=MESH
        )

    for copy in consts + loads:
        copy.start()
    for copy in own_a:
        copy.start()
    pl.semaphore_wait(barrier, SLOTS - 1 + SECTORS - 1)

    for g in range(count):
        for k in range(1, SLOTS):
            send_a(g, k).start()
    for copy in halos[0]:
        copy.start()

    cutoff = jnp.maximum(4, lax.div(POINTS * (sp + 1), 2 * NEAR))
    width = 2 * cutoff - 1
    weight = 1.0 - sp.astype(jnp.float32) / NEAR

    @pl.loop(0, POINTS // 32)
    def _(b):
        row = lax.broadcasted_iota(jnp.int32, (32, POINTS), 0) + b * 32
        col = lax.broadcasted_iota(jnp.int32, (32, POINTS), 1)
        gap = (row - col + POINTS) & (POINTS - 1)
        top = jnp.sin(((gap * width) & (2 * POINTS - 1)).astype(jnp.float32) * (np.pi / POINTS))
        low = jnp.sin(gap.astype(jnp.float32) * (np.pi / POINTS))
        same = gap == 0
        ratio = top / jnp.where(same, 1.0, low)
        table = jnp.where(same, width.astype(jnp.float32), ratio) * (1.0 / POINTS)
        mtab[pl.ds(pl.multiple_of(b * 32, 32), 32), :] = weight * table + jnp.where(
            same, 1.0 - weight, 0.0
        )

    def mix(g):
        own_a[g].wait()
        for k in range(1, SLOTS):
            arrive_a(g, k).wait_recv()
        fields = bounds[g][1] - bounds[g][0]
        coef = {
            (j, n): tab[imap[j] - imap[n] + SLOTS - 1]
            for n in range(SLOTS)
            for j in range(n + 1, SLOTS)
        }

        @pl.loop(0, fields * NEAR // 8)
        def _(b):
            fi, r0 = lax.div(b, NEAR // 8), lax.rem(b, NEAR // 8) * 8
            block = pl.ds(pl.multiple_of(r0, 8), 8)
            values = [recv_a[g][j, fi, block, :] for j in range(SLOTS)]
            for n in range(SLOTS):
                total = None
                for j in range(SLOTS):
                    if j == n:
                        continue
                    term = coef[max(j, n), min(j, n)] * values[j]
                    if total is None:
                        total = term if j > n else -term
                    else:
                        total = total + term if j > n else total - term
                mixed[g][n, fi, block, :] = total

        for k in range(1, SLOTS):
            send_c(g, k).start()
        own_c[g].start()

    for copy in consts:
        copy.wait()
    for g in range(count):
        mix(g)

    for copy in loads:
        copy.wait()
    for copy in halos[0]:
        copy.wait_recv()

    window = NEAR + 8
    shape = (window, CELLS_X)
    col = lax.broadcasted_iota(jnp.int32, shape, 1)

    def stencil(part):
        base = part * (CYCLES - window)
        span = pl.ds(base, window)
        keep = slice(8 * part, 8 * part + NEAR)
        target = pl.ds(part * NEAR, NEAR)
        row = lax.broadcasted_iota(jnp.int32, shape, 0) + base

        @pl.loop(0, SECTOR)
        def _(t):
            mu = mux[t + 1, span]
            half_cycle = 0.5 / (row[keep].astype(jnp.float32) + 1.0)
            up = half_cycle * (mu[keep] + mux[t + 2, target])
            down = half_cycle * (mu[keep] + mux[t, target])
            out_r = jnp.where(
                row < CYCLES - 1, 0.5 * (mu + pltpu.roll(mu, window - 1, 0)), 0.0
            )
            in_r = jnp.where(row > 0, pltpu.roll(out_r, 1, 0), 0.0)
            out_x = jnp.where(
                col < CELLS_X - 1, 0.5 * (mu + pltpu.roll(mu, CELLS_X - 1, 1)), 0.0
            )
            in_x = pltpu.roll(out_x, 1, 1)
            own = up + down + (out_r + in_r + out_x + in_x)[keep]
            for f in range(FIELDS):
                p = adjx[f, t + 1, span]
                face = [1.0 - bcf[i, f].astype(jnp.float32) for i in range(3)]
                edge = (
                    jnp.where(row[keep] == CYCLES - 1, face[2], 0.0)
                    + jnp.where(col[keep] == 0, face[0], 0.0)
                    + jnp.where(col[keep] == CELLS_X - 1, face[1], 0.0)
                )
                core = p[keep]
                diffused = (own + edge * mu[keep]) * core
                diffused = diffused - up * adjx[f, t + 2, target] - down * adjx[f, t, target]
                diffused = diffused - (out_r * pltpu.roll(p, window - 1, 0))[keep]
                diffused = diffused - (in_r * pltpu.roll(p, 1, 0))[keep]
                diffused = diffused - out_x[keep] * pltpu.roll(core, CELLS_X - 1, 1)
                diffused = diffused - in_x[keep] * pltpu.roll(core, 1, 1)
                total = local[f, t, target] + kap[f] * diffused
                for g in range(FIELDS):
                    total = total + cpl[g, f] * adjx[g, t + 1, target]
                local[f, t, target] = total

    stencil(0)

    for g in range(count):
        lo, hi, _ = bounds[g]
        own_c[g].wait()
        for k in range(1, SLOTS):
            arrive_c(g, k).wait_recv()
        stride = (hi - lo) * SECTOR

        @pl.loop(0, SECTOR)
        def _(t):
            for f in range(lo, hi):
                for b in range(NEAR // 8):
                    block = pl.ds(b * 8, 8)
                    value = local[f, t, block, :] + spec[g][f - lo, t, block, :]
                    start = b * 8 * stride + (f - lo) * SECTOR + t
                    stage_e[g][pl.ds(start, 8, stride=stride), :] = value

        own_e[g].start()

        for i in range(1, SECTORS):
            send_s(stage_e, recv_e, e_send, e_recv, g, SECTORS - i, sp).start()

    for k in range(1, SLOTS):
        send_a(count, k).start()
    for copy in halos[1]:
        copy.start()
    for copy in halos[1]:
        copy.wait_recv()
    stencil(1)

    for g in range(count):
        lo, hi, _ = bounds[g]
        if g == count - 1:
            mix(count)
        own_e[g].wait()

        for i in range(1, SECTORS):
            send_s(
                stage_e, recv_e, e_send, e_recv, g, SECTORS - i, sp
            ).wait_recv()

        pencils = recv_e[g][...].reshape(SECTORS, (hi - lo) * SECTOR, CELLS_X)
        parts = []
        for f in range(hi - lo):
            pencil = pencils[:, f * SECTOR : (f + 1) * SECTOR, :].reshape(POINTS, CELLS_X)
            smooth = jnp.dot(
                mtab[...],
                pencil,
                precision=lax.Precision.HIGHEST,
                preferred_element_type=jnp.float32,
            )
            parts.append(smooth.reshape(SECTORS, SECTOR, CELLS_X))
        stage_g[g][...] = jnp.concatenate(parts, axis=1).reshape(
            SECTORS * (hi - lo) * SECTOR, CELLS_X
        )
        own_g[g].start()

        for i in range(1, SECTORS):
            send_s(stage_g, recv_g, g_send, g_recv, g, SECTORS - i, sp).start()

    own_c[count].wait()
    for k in range(1, SLOTS):
        arrive_c(count, k).wait_recv()

    @pl.loop(0, SECTOR)
    def _(t):
        for f in range(FIELDS):
            out[0, f, t, pl.ds(NEAR, NEAR), :] = (
                local[f, t, pl.ds(NEAR, NEAR), :] + spec[count][f, t]
            )

    for g in range(count):
        lo, hi, _ = bounds[g]
        own_g[g].wait()

        for i in range(1, SECTORS):
            send_s(
                stage_g, recv_g, g_send, g_recv, g, SECTORS - i, sp
            ).wait_recv()

        stride = (hi - lo) * SECTOR

        @pl.loop(0, SECTOR)
        def _(t):
            for f in range(lo, hi):
                for b in range(NEAR // 8):
                    start = b * 8 * stride + (f - lo) * SECTOR + t
                    out[0, f, t, pl.ds(b * 8, 8), :] = recv_g[g][
                        pl.ds(start, 8, stride=stride), :
                    ]

    for copy in halos[0] + halos[1]:
        copy.wait_send()
    for g in range(count + 1):
        for k in range(1, SLOTS):
            send_a(g, k).wait_send()
            send_c(g, k).wait_send()
    for g in range(count):

        for i in range(1, SECTORS):
            send_s(stage_e, recv_e, e_send, e_recv, g, SECTORS - i, sp).wait_send()
            send_s(stage_g, recv_g, g_send, g_recv, g, SECTORS - i, sp).wait_send()


def body(adjoint, source, viscosity, kappa, coupling, bc_flags, inst_map):
    count = len(GROUPS)
    sizes = [hi - lo for lo, hi in GROUPS]
    f32 = jnp.float32
    vmem, dma = pltpu.VMEM, pltpu.SemaphoreType.DMA
    slabs = [vmem((SLOTS, n, NEAR, CELLS_X), f32) for n in sizes + [FIELDS]]
    sectors = [vmem((n, SECTOR, NEAR, CELLS_X), f32) for n in sizes + [FIELDS]]
    pencils = [vmem((SECTORS * n * SECTOR, CELLS_X), f32) for n in sizes]
    scratch = [
        vmem((FIELDS, SECTOR + 2, CYCLES, CELLS_X), f32),
        vmem((SECTOR + 2, CYCLES, CELLS_X), f32),
        vmem((FIELDS, SECTOR, CYCLES, CELLS_X), f32),
        vmem((POINTS, POINTS), f32),
        *slabs,
        *slabs,
        *sectors,
        *(pencils * 4),
        dma((8,)),
        dma((8,)),
        dma((8,)),
        dma((4, count + 1)),
        *[
            pltpu.SMEM(x.shape, x.dtype)
            for x in (kappa, coupling, bc_flags.T, inst_map, slot_table())
        ],
        *[dma((count + 1, SLOTS))] * 4,
        *[dma((count, SECTORS))] * 4,
    ]
    hbm = pl.BlockSpec(memory_space=pltpu.HBM)
    return pl.pallas_call(
        kernel,
        out_shape=jax.ShapeDtypeStruct(adjoint.shape, f32),
        in_specs=[hbm] * 8,
        out_specs=pl.BlockSpec(memory_space=pltpu.VMEM),
        scratch_shapes=scratch,
        compiler_params=pltpu.CompilerParams(
            collective_id=0, has_side_effects=True, vmem_limit_bytes=48 * 1024 * 1024
        ),
        name="residual",
    )(*[
        pltpu.with_memory_space_constraint(x, pltpu.HBM)
        for x in (
            adjoint, source, viscosity, kappa, coupling, bc_flags.T, inst_map, slot_table()
        )
    ])


def solution(mesh):
    return jax.shard_map(
        body,
        mesh=mesh,
        in_specs=(
            P("inst", None, "space", None, None),
            P("inst", None, "space", None, None),
            P("space", None, None),
            P(),
            P(),
            P(),
            P(),
        ),
        out_specs=P("inst", None, "space", None, None),
        check_vma=False,
    )
```

```python
import functools

import jax
import jax.numpy as jnp
import numpy as np
from jax import lax
from jax.experimental import pallas as pl
from jax.experimental.pallas import tpu as pltpu
from jax.sharding import PartitionSpec as P

FIELDS, SECTOR, CYCLES, CELLS_X = 5, 8, 64, 128
POINTS, NEAR, SLOTS, SECTORS = 256, 32, 8, 32
GROUPS = ((0, 2), (2, 5))
MESH = pl.DeviceIdType.MESH


def slot_table():
    offset = np.arange(-(SLOTS - 1), SLOTS + 1)
    parity = 1.0 - 2.0 * (np.abs(offset) % 2)
    sines = np.sin(np.pi * offset / SLOTS)
    inner = (offset != 0) & (np.abs(offset) < SLOTS)
    table = np.where(inner, 0.5 * parity / np.where(inner, sines, 1.0), 0.0)
    return jnp.asarray(table.astype(np.float32))


def kernel(adj, src, visc, *refs):
    smalls, out, scratch = refs[:5], refs[5], refs[6:]
    count = len(GROUPS)
    names = iter(scratch)
    take = lambda n: [next(names) for _ in range(n)]
    adjx, mux, local, mtab = take(4)
    recv_a = take(count + 1)
    mixed = take(count + 1)
    spec = take(count + 1)
    stage_e, recv_e, stage_g, recv_g = take(count), take(count), take(count), take(count)
    load_sem, halo_send, halo_recv, own_sem, ready = take(5)
    held = take(5)
    kap, cpl, bcf, imap, tab = held
    a_send, a_recv, c_send, c_recv = take(4)
    e_send, e_recv, g_send, g_recv = take(4)

    me, sp = lax.axis_index("inst"), lax.axis_index("space")
    ix, iy = lax.div(me, 2), lax.rem(me, 2)
    sz, sy, sc = lax.div(sp, 4), lax.rem(lax.div(sp, 2), 2), lax.rem(sp, 2)

    flip_y = [iy, lax.rem(iy + 1, 2)]
    turn_x = [lax.rem(ix + k, 4) * 2 for k in range(4)]
    turn_z = [lax.rem(sz + k, 8) * 4 for k in range(8)]
    flip_s = [sy * 2, lax.rem(sy + 1, 2) * 2]
    flip_c = [sc, lax.rem(sc + 1, 2)]

    def inst_at(k, sign):
        return turn_x[(sign * (k // 2)) % 4] + flip_y[k % 2]

    def space_at(i, sign):
        step = i // 4
        kz = (step + 1) // 2 * (1 - 2 * (step % 2))
        return turn_z[(sign * kz) % 8] + flip_s[i // 2 % 2] + flip_c[i % 2]

    loads = [
        pltpu.make_async_copy(visc, mux.at[pl.ds(1, SECTOR)], load_sem.at[0]),
        pltpu.make_async_copy(adj.at[0], adjx.at[:, pl.ds(1, SECTOR)], load_sem.at[1]),
        pltpu.make_async_copy(src.at[0], local, load_sem.at[2]),
    ]
    consts = [
        pltpu.make_async_copy(small, ref, load_sem.at[3 + i])
        for i, (small, ref) in enumerate(zip(smalls, held))
    ]
    bounds = [(lo, hi, 0) for lo, hi in GROUPS] + [(0, FIELDS, NEAR)]

    def chunk(g, slot):
        lo, hi, first = bounds[g]
        return adj.at[0, pl.ds(lo, hi - lo), slot, pl.ds(first, NEAR), :]

    own_a = [
        pltpu.make_async_copy(chunk(g, me), recv_a[g].at[me], own_sem.at[0, g])
        for g in range(count + 1)
    ]
    own_c = [
        pltpu.make_async_copy(mixed[g].at[me], spec[g].at[:, me], own_sem.at[1, g])
        for g in range(count + 1)
    ]

    def rows(g, index):
        depth = (bounds[g][1] - bounds[g][0]) * SECTOR
        return pl.ds(pl.multiple_of(index * depth, 8), depth)

    own_e = [
        pltpu.make_async_copy(
            stage_e[g].at[rows(g, sp)], recv_e[g].at[rows(g, sp)], own_sem.at[2, g]
        )
        for g in range(count)
    ]
    own_g = [
        pltpu.make_async_copy(
            stage_g[g].at[rows(g, sp)], recv_g[g].at[rows(g, sp)], own_sem.at[3, g]
        )
        for g in range(count)
    ]

    def send_a(g, k):
        return pltpu.make_async_remote_copy(
            src_ref=chunk(g, inst_at(k, 1)),
            dst_ref=recv_a[g].at[me],
            send_sem=a_send.at[g, k],
            recv_sem=a_recv.at[g, k],
            device_id={"inst": inst_at(k, 1)},
            device_id_type=MESH,
        )

    def arrive_a(g, k):
        return pltpu.make_async_remote_copy(
            src_ref=chunk(g, me),
            dst_ref=recv_a[g].at[inst_at(k, -1)],
            send_sem=a_send.at[g, k],
            recv_sem=a_recv.at[g, k],
            device_id={"inst": inst_at(k, 1)},
            device_id_type=MESH,
        )

    def send_c(g, k):
        return pltpu.make_async_remote_copy(
            src_ref=mixed[g].at[inst_at(k, 1)],
            dst_ref=spec[g].at[:, me],
            send_sem=c_send.at[g, k],
            recv_sem=c_recv.at[g, k],
            device_id={"inst": inst_at(k, 1)},
            device_id_type=MESH,
        )

    def arrive_c(g, k):
        return pltpu.make_async_remote_copy(
            src_ref=mixed[g].at[me],
            dst_ref=spec[g].at[:, inst_at(k, -1)],
            send_sem=c_send.at[g, k],
            recv_sem=c_recv.at[g, k],
            device_id={"inst": inst_at(k, 1)},
            device_id_type=MESH,
        )

    def send_s(stage, recv, send_sem, recv_sem, g, i, slot):
        return pltpu.make_async_remote_copy(
            src_ref=stage[g].at[rows(g, space_at(i, 1))],
            dst_ref=recv[g].at[rows(g, slot)],
            send_sem=send_sem.at[g, i],
            recv_sem=recv_sem.at[g, i],
            device_id={"space": space_at(i, 1)},
            device_id_type=MESH,
        )

    after, before = lax.rem(sp + 1, SECTORS), lax.rem(sp + SECTORS - 1, SECTORS)

    def halo(index, source, target, peer):
        return pltpu.make_async_remote_copy(
            src_ref=source,
            dst_ref=target,
            send_sem=halo_send.at[index],
            recv_sem=halo_recv.at[index],
            device_id={"space": peer},
            device_id_type=MESH,
        )

    def halos_of(part):
        span = pl.ds(part * NEAR, NEAR)
        first, last = SECTOR - 1, SECTOR + 1
        return [
            halo(4 * part, adj.at[0, :, first, span], adjx.at[:, 0, span], after),
            halo(4 * part + 1, adj.at[0, :, 0, span], adjx.at[:, last, span], before),
            halo(4 * part + 2, visc.at[first, span], mux.at[0, span], after),
            halo(4 * part + 3, visc.at[0, span], mux.at[last, span], before),
        ]

    halos = [halos_of(0), halos_of(1)]

    barrier = pltpu.get_barrier_semaphore()
    for k in range(1, SLOTS):
        pl.semaphore_signal(
            barrier, inc=1, device_id={"inst": inst_at(k, 1)}, device_id_type=MESH
        )

    for peer in (after, before):
        pl.semaphore_signal(barrier, inc=1, device_id={"space": peer}, device_id_type=MESH)

    def greet(j):
        for sign in (1, -1):
            peer = lax.rem(sp + sign * 2**j + SECTORS, SECTORS)
            pl.semaphore_signal(
                ready.at[j], inc=1, device_id={"space": peer}, device_id_type=MESH
            )

    def met(j):
        pl.semaphore_wait(ready.at[j], 2)

    for copy in consts + loads:
        copy.start()
    for copy in own_a:
        copy.start()
    pl.semaphore_wait(barrier, SLOTS - 1 + 2)
    greet(0)

    for g in range(count):
        for k in range(1, SLOTS):
            send_a(g, k).start()
    for copy in halos[0]:
        copy.start()

    cutoff = jnp.maximum(4, lax.div(POINTS * (sp + 1), 2 * NEAR))
    width = 2 * cutoff - 1
    weight = 1.0 - sp.astype(jnp.float32) / NEAR

    @pl.loop(0, POINTS // 32)
    def _(b):
        row = lax.broadcasted_iota(jnp.int32, (32, POINTS), 0) + b * 32
        col = lax.broadcasted_iota(jnp.int32, (32, POINTS), 1)
        gap = (row - col + POINTS) & (POINTS - 1)
        top = jnp.sin(((gap * width) & (2 * POINTS - 1)).astype(jnp.float32) * (np.pi / POINTS))
        low = jnp.sin(gap.astype(jnp.float32) * (np.pi / POINTS))
        same = gap == 0
        ratio = top / jnp.where(same, 1.0, low)
        table = jnp.where(same, width.astype(jnp.float32), ratio) * (1.0 / POINTS)
        mtab[pl.ds(pl.multiple_of(b * 32, 32), 32), :] = weight * table + jnp.where(
            same, 1.0 - weight, 0.0
        )

    def mix(g):
        own_a[g].wait()
        for k in range(1, SLOTS):
            arrive_a(g, k).wait_recv()
        fields = bounds[g][1] - bounds[g][0]
        coef = {
            (j, n): tab[imap[j] - imap[n] + SLOTS - 1]
            for n in range(SLOTS)
            for j in range(n + 1, SLOTS)
        }

        @pl.loop(0, fields * NEAR // 8)
        def _(b):
            fi, r0 = lax.div(b, NEAR // 8), lax.rem(b, NEAR // 8) * 8
            block = pl.ds(pl.multiple_of(r0, 8), 8)
            values = [recv_a[g][j, fi, block, :] for j in range(SLOTS)]
            for n in range(SLOTS):
                total = None
                for j in range(SLOTS):
                    if j == n:
                        continue
                    term = coef[max(j, n), min(j, n)] * values[j]
                    if total is None:
                        total = term if j > n else -term
                    else:
                        total = total + term if j > n else total - term
                mixed[g][n, fi, block, :] = total

        for k in range(1, SLOTS):
            send_c(g, k).start()
        own_c[g].start()

    for copy in consts:
        copy.wait()
    met(0)
    greet(1)
    for g in range(count):
        mix(g)
        if g == 0:
            met(1)
            greet(2)

    for copy in loads:
        copy.wait()
    for copy in halos[0]:
        copy.wait_recv()

    window = NEAR + 8
    shape = (window, CELLS_X)
    col = lax.broadcasted_iota(jnp.int32, shape, 1)

    def stencil(part):
        base = part * (CYCLES - window)
        span = pl.ds(base, window)
        keep = slice(8 * part, 8 * part + NEAR)
        target = pl.ds(part * NEAR, NEAR)
        row = lax.broadcasted_iota(jnp.int32, shape, 0) + base

        @pl.loop(0, SECTOR)
        def _(t):
            mu = mux[t + 1, span]
            half_cycle = 0.5 / (row[keep].astype(jnp.float32) + 1.0)
            up = half_cycle * (mu[keep] + mux[t + 2, target])
            down = half_cycle * (mu[keep] + mux[t, target])
            out_r = jnp.where(
                row < CYCLES - 1, 0.5 * (mu + pltpu.roll(mu, window - 1, 0)), 0.0
            )
            in_r = jnp.where(row > 0, pltpu.roll(out_r, 1, 0), 0.0)
            out_x = jnp.where(
                col < CELLS_X - 1, 0.5 * (mu + pltpu.roll(mu, CELLS_X - 1, 1)), 0.0
            )
            in_x = pltpu.roll(out_x, 1, 1)
            own = up + down + (out_r + in_r + out_x + in_x)[keep]
            for f in range(FIELDS):
                p = adjx[f, t + 1, span]
                face = [1.0 - bcf[i, f].astype(jnp.float32) for i in range(3)]
                edge = (
                    jnp.where(row[keep] == CYCLES - 1, face[2], 0.0)
                    + jnp.where(col[keep] == 0, face[0], 0.0)
                    + jnp.where(col[keep] == CELLS_X - 1, face[1], 0.0)
                )
                core = p[keep]
                diffused = (own + edge * mu[keep]) * core
                diffused = diffused - up * adjx[f, t + 2, target] - down * adjx[f, t, target]
                diffused = diffused - (out_r * pltpu.roll(p, window - 1, 0))[keep]
                diffused = diffused - (in_r * pltpu.roll(p, 1, 0))[keep]
                diffused = diffused - out_x[keep] * pltpu.roll(core, CELLS_X - 1, 1)
                diffused = diffused - in_x[keep] * pltpu.roll(core, 1, 1)
                total = local[f, t, target] + kap[f] * diffused
                for g in range(FIELDS):
                    total = total + cpl[g, f] * adjx[g, t + 1, target]
                local[f, t, target] = total

    stencil(0)
    met(2)
    greet(3)

    for g in range(count):
        lo, hi, _ = bounds[g]
        own_c[g].wait()
        for k in range(1, SLOTS):
            arrive_c(g, k).wait_recv()
        stride = (hi - lo) * SECTOR

        @pl.loop(0, SECTOR)
        def _(t):
            for f in range(lo, hi):
                for b in range(NEAR // 8):
                    block = pl.ds(b * 8, 8)
                    value = local[f, t, block, :] + spec[g][f - lo, t, block, :]
                    start = b * 8 * stride + (f - lo) * SECTOR + t
                    stage_e[g][pl.ds(start, 8, stride=stride), :] = value

        if g == 0:
            met(3)
        own_e[g].start()

        for i in range(1, SECTORS):
            send_s(stage_e, recv_e, e_send, e_recv, g, SECTORS - i, sp).start()

    for copy in halos[1]:
        copy.start()
    for k in range(1, SLOTS):
        send_a(count, k).start()

    for g in range(count):
        lo, hi, _ = bounds[g]
        own_e[g].wait()

        for i in range(1, SECTORS):
            send_s(
                stage_e, recv_e, e_send, e_recv, g, SECTORS - i, sp
            ).wait_recv()

        pencils = recv_e[g][...].reshape(SECTORS, (hi - lo) * SECTOR, CELLS_X)
        parts = []
        for f in range(hi - lo):
            pencil = pencils[:, f * SECTOR : (f + 1) * SECTOR, :].reshape(POINTS, CELLS_X)
            smooth = jnp.dot(
                mtab[...],
                pencil,
                precision=lax.Precision.HIGHEST,
                preferred_element_type=jnp.float32,
            )
            parts.append(smooth.reshape(SECTORS, SECTOR, CELLS_X))
        stage_g[g][...] = jnp.concatenate(parts, axis=1).reshape(
            SECTORS * (hi - lo) * SECTOR, CELLS_X
        )
        own_g[g].start()

        for i in range(1, SECTORS):
            send_s(stage_g, recv_g, g_send, g_recv, g, SECTORS - i, sp).start()

    mix(count)
    for copy in halos[1]:
        copy.wait_recv()
    stencil(1)
    own_c[count].wait()
    for k in range(1, SLOTS):
        arrive_c(count, k).wait_recv()

    @pl.loop(0, SECTOR)
    def _(t):
        for f in range(FIELDS):
            out[0, f, t, pl.ds(NEAR, NEAR), :] = (
                local[f, t, pl.ds(NEAR, NEAR), :] + spec[count][f, t]
            )

    for g in range(count):
        lo, hi, _ = bounds[g]
        own_g[g].wait()

        for i in range(1, SECTORS):
            send_s(
                stage_g, recv_g, g_send, g_recv, g, SECTORS - i, sp
            ).wait_recv()

        stride = (hi - lo) * SECTOR

        @pl.loop(0, SECTOR)
        def _(t):
            for f in range(lo, hi):
                for b in range(NEAR // 8):
                    start = b * 8 * stride + (f - lo) * SECTOR + t
                    out[0, f, t, pl.ds(b * 8, 8), :] = recv_g[g][
                        pl.ds(start, 8, stride=stride), :
                    ]

    for copy in halos[0] + halos[1]:
        copy.wait_send()
    for g in range(count + 1):
        for k in range(1, SLOTS):
            send_a(g, k).wait_send()
            send_c(g, k).wait_send()
    for g in range(count):

        for i in range(1, SECTORS):
            send_s(stage_e, recv_e, e_send, e_recv, g, SECTORS - i, sp).wait_send()
            send_s(stage_g, recv_g, g_send, g_recv, g, SECTORS - i, sp).wait_send()


def body(adjoint, source, viscosity, kappa, coupling, bc_flags, inst_map):
    count = len(GROUPS)
    sizes = [hi - lo for lo, hi in GROUPS]
    f32 = jnp.float32
    vmem, dma = pltpu.VMEM, pltpu.SemaphoreType.DMA
    slabs = [vmem((SLOTS, n, NEAR, CELLS_X), f32) for n in sizes + [FIELDS]]
    sectors = [vmem((n, SECTOR, NEAR, CELLS_X), f32) for n in sizes + [FIELDS]]
    pencils = [vmem((SECTORS * n * SECTOR, CELLS_X), f32) for n in sizes]
    scratch = [
        vmem((FIELDS, SECTOR + 2, CYCLES, CELLS_X), f32),
        vmem((SECTOR + 2, CYCLES, CELLS_X), f32),
        vmem((FIELDS, SECTOR, CYCLES, CELLS_X), f32),
        vmem((POINTS, POINTS), f32),
        *slabs,
        *slabs,
        *sectors,
        *(pencils * 4),
        dma((8,)),
        dma((8,)),
        dma((8,)),
        dma((4, count + 1)),
        pltpu.SemaphoreType.REGULAR((4,)),
        *[
            pltpu.SMEM(x.shape, x.dtype)
            for x in (kappa, coupling, bc_flags.T, inst_map, slot_table())
        ],
        *[dma((count + 1, SLOTS))] * 4,
        *[dma((count, SECTORS))] * 4,
    ]
    hbm = pl.BlockSpec(memory_space=pltpu.HBM)
    return pl.pallas_call(
        kernel,
        out_shape=jax.ShapeDtypeStruct(adjoint.shape, f32),
        in_specs=[hbm] * 8,
        out_specs=pl.BlockSpec(memory_space=pltpu.VMEM),
        scratch_shapes=scratch,
        compiler_params=pltpu.CompilerParams(
            collective_id=0, has_side_effects=True, vmem_limit_bytes=48 * 1024 * 1024
        ),
        name="residual",
    )(*[
        pltpu.with_memory_space_constraint(x, pltpu.HBM)
        for x in (
            adjoint, source, viscosity, kappa, coupling, bc_flags.T, inst_map, slot_table()
        )
    ])


def solution(mesh):
    return jax.shard_map(
        body,
        mesh=mesh,
        in_specs=(
            P("inst", None, "space", None, None),
            P("inst", None, "space", None, None),
            P("space", None, None),
            P(),
            P(),
            P(),
            P(),
        ),
        out_specs=P("inst", None, "space", None, None),
        check_vma=False,
    )
```

```python
import functools

import jax
import jax.numpy as jnp
import numpy as np
from jax import lax
from jax.experimental import pallas as pl
from jax.experimental.pallas import tpu as pltpu
from jax.sharding import PartitionSpec as P

FIELDS, SECTOR, CYCLES, CELLS_X = 5, 8, 64, 128
POINTS, NEAR, SLOTS, SECTORS = 256, 32, 8, 32
GROUPS = ((0, 2), (2, 5))
MESH = pl.DeviceIdType.MESH


def slot_table():
    offset = np.arange(-(SLOTS - 1), SLOTS + 1)
    parity = 1.0 - 2.0 * (np.abs(offset) % 2)
    sines = np.sin(np.pi * offset / SLOTS)
    inner = (offset != 0) & (np.abs(offset) < SLOTS)
    table = np.where(inner, 0.5 * parity / np.where(inner, sines, 1.0), 0.0)
    return jnp.asarray(table.astype(np.float32))


def kernel(adj, src, visc, *refs):
    smalls, out, scratch = refs[:5], refs[5], refs[6:]
    count = len(GROUPS)
    names = iter(scratch)
    take = lambda n: [next(names) for _ in range(n)]
    adjx, mux, local, mtab = take(4)
    recv_a = take(count + 1)
    mixed = take(count + 1)
    spec = take(count + 1)
    stage_e, recv_e, stage_g, recv_g = take(count), take(count), take(count), take(count)
    load_sem, halo_send, halo_recv, own_sem, ready = take(5)
    held = take(5)
    kap, cpl, bcf, imap, tab = held
    a_send, a_recv, c_send, c_recv = take(4)
    e_send, e_recv, g_send, g_recv = take(4)

    me, sp = lax.axis_index("inst"), lax.axis_index("space")
    ix, iy = lax.div(me, 2), lax.rem(me, 2)
    sz, sy, sc = lax.div(sp, 4), lax.rem(lax.div(sp, 2), 2), lax.rem(sp, 2)

    flip_y = [iy, lax.rem(iy + 1, 2)]
    turn_x = [lax.rem(ix + k, 4) * 2 for k in range(4)]
    turn_z = [lax.rem(sz + k, 8) * 4 for k in range(8)]
    flip_s = [sy * 2, lax.rem(sy + 1, 2) * 2]
    flip_c = [sc, lax.rem(sc + 1, 2)]

    def inst_at(k, sign):
        return turn_x[(sign * (k // 2)) % 4] + flip_y[k % 2]

    def space_at(i, sign):
        step = i // 2 % 8
        kz = (step + 1) // 2 * (1 - 2 * (step % 2))
        return turn_z[(sign * kz) % 8] + flip_s[i // 16] + flip_c[i % 2]

    loads = [
        pltpu.make_async_copy(visc, mux.at[pl.ds(1, SECTOR)], load_sem.at[0]),
        pltpu.make_async_copy(adj.at[0], adjx.at[:, pl.ds(1, SECTOR)], load_sem.at[1]),
        pltpu.make_async_copy(src.at[0], local, load_sem.at[2]),
    ]
    consts = [
        pltpu.make_async_copy(small, ref, load_sem.at[3 + i])
        for i, (small, ref) in enumerate(zip(smalls, held))
    ]
    bounds = [(lo, hi, 0) for lo, hi in GROUPS] + [(0, FIELDS, NEAR)]

    def chunk(g, slot):
        lo, hi, first = bounds[g]
        return adj.at[0, pl.ds(lo, hi - lo), slot, pl.ds(first, NEAR), :]

    own_a = [
        pltpu.make_async_copy(chunk(g, me), recv_a[g].at[me], own_sem.at[0, g])
        for g in range(count + 1)
    ]
    own_c = [
        pltpu.make_async_copy(mixed[g].at[me], spec[g].at[:, me], own_sem.at[1, g])
        for g in range(count + 1)
    ]

    def rows(g, index):
        depth = (bounds[g][1] - bounds[g][0]) * SECTOR
        return pl.ds(pl.multiple_of(index * depth, 8), depth)

    own_e = [
        pltpu.make_async_copy(
            stage_e[g].at[rows(g, sp)], recv_e[g].at[rows(g, sp)], own_sem.at[2, g]
        )
        for g in range(count)
    ]
    own_g = [
        pltpu.make_async_copy(
            stage_g[g].at[rows(g, sp)], recv_g[g].at[rows(g, sp)], own_sem.at[3, g]
        )
        for g in range(count)
    ]

    def send_a(g, k):
        return pltpu.make_async_remote_copy(
            src_ref=chunk(g, inst_at(k, 1)),
            dst_ref=recv_a[g].at[me],
            send_sem=a_send.at[g, k],
            recv_sem=a_recv.at[g, k],
            device_id={"inst": inst_at(k, 1)},
            device_id_type=MESH,
        )

    def arrive_a(g, k):
        return pltpu.make_async_remote_copy(
            src_ref=chunk(g, me),
            dst_ref=recv_a[g].at[inst_at(k, -1)],
            send_sem=a_send.at[g, k],
            recv_sem=a_recv.at[g, k],
            device_id={"inst": inst_at(k, 1)},
            device_id_type=MESH,
        )

    def send_c(g, k):
        return pltpu.make_async_remote_copy(
            src_ref=mixed[g].at[inst_at(k, 1)],
            dst_ref=spec[g].at[:, me],
            send_sem=c_send.at[g, k],
            recv_sem=c_recv.at[g, k],
            device_id={"inst": inst_at(k, 1)},
            device_id_type=MESH,
        )

    def arrive_c(g, k):
        return pltpu.make_async_remote_copy(
            src_ref=mixed[g].at[me],
            dst_ref=spec[g].at[:, inst_at(k, -1)],
            send_sem=c_send.at[g, k],
            recv_sem=c_recv.at[g, k],
            device_id={"inst": inst_at(k, 1)},
            device_id_type=MESH,
        )

    def send_s(stage, recv, send_sem, recv_sem, g, i, slot):
        return pltpu.make_async_remote_copy(
            src_ref=stage[g].at[rows(g, space_at(i, 1))],
            dst_ref=recv[g].at[rows(g, slot)],
            send_sem=send_sem.at[g, i],
            recv_sem=recv_sem.at[g, i],
            device_id={"space": space_at(i, 1)},
            device_id_type=MESH,
        )

    after, before = lax.rem(sp + 1, SECTORS), lax.rem(sp + SECTORS - 1, SECTORS)

    def halo(index, source, target, peer):
        return pltpu.make_async_remote_copy(
            src_ref=source,
            dst_ref=target,
            send_sem=halo_send.at[index],
            recv_sem=halo_recv.at[index],
            device_id={"space": peer},
            device_id_type=MESH,
        )

    def halos_of(part):
        span = pl.ds(part * NEAR, NEAR)
        first, last = SECTOR - 1, SECTOR + 1
        return [
            halo(4 * part, adj.at[0, :, first, span], adjx.at[:, 0, span], after),
            halo(4 * part + 1, adj.at[0, :, 0, span], adjx.at[:, last, span], before),
            halo(4 * part + 2, visc.at[first, span], mux.at[0, span], after),
            halo(4 * part + 3, visc.at[0, span], mux.at[last, span], before),
        ]

    halos = [halos_of(0), halos_of(1)]

    barrier = pltpu.get_barrier_semaphore()
    for k in range(1, SLOTS):
        pl.semaphore_signal(
            barrier, inc=1, device_id={"inst": inst_at(k, 1)}, device_id_type=MESH
        )

    for peer in (after, before):
        pl.semaphore_signal(barrier, inc=1, device_id={"space": peer}, device_id_type=MESH)

    def greet(j):
        for sign in (1, -1):
            peer = lax.rem(sp + sign * 2**j + SECTORS, SECTORS)
            pl.semaphore_signal(
                ready.at[j], inc=1, device_id={"space": peer}, device_id_type=MESH
            )

    def met(j):
        pl.semaphore_wait(ready.at[j], 2)

    for copy in consts + loads:
        copy.start()
    for copy in own_a:
        copy.start()
    pl.semaphore_wait(barrier, SLOTS - 1 + 2)
    greet(0)

    for g in range(count):
        for k in (5, 3, 7, 1, 4, 2, 6):
            send_a(g, k).start()
    for copy in halos[0]:
        copy.start()

    cutoff = jnp.maximum(4, lax.div(POINTS * (sp + 1), 2 * NEAR))
    width = 2 * cutoff - 1
    weight = 1.0 - sp.astype(jnp.float32) / NEAR

    @pl.loop(0, POINTS // 32)
    def _(b):
        row = lax.broadcasted_iota(jnp.int32, (32, POINTS), 0) + b * 32
        col = lax.broadcasted_iota(jnp.int32, (32, POINTS), 1)
        gap = (row - col + POINTS) & (POINTS - 1)
        top = jnp.sin(((gap * width) & (2 * POINTS - 1)).astype(jnp.float32) * (np.pi / POINTS))
        low = jnp.sin(gap.astype(jnp.float32) * (np.pi / POINTS))
        same = gap == 0
        ratio = top / jnp.where(same, 1.0, low)
        table = jnp.where(same, width.astype(jnp.float32), ratio) * (1.0 / POINTS)
        mtab[pl.ds(pl.multiple_of(b * 32, 32), 32), :] = weight * table + jnp.where(
            same, 1.0 - weight, 0.0
        )

    def mix(g):
        own_a[g].wait()
        for k in range(1, SLOTS):
            arrive_a(g, k).wait_recv()
        fields = bounds[g][1] - bounds[g][0]
        coef = {
            (j, n): tab[imap[j] - imap[n] + SLOTS - 1]
            for n in range(SLOTS)
            for j in range(n + 1, SLOTS)
        }

        @pl.loop(0, fields * NEAR // 8)
        def _(b):
            fi, r0 = lax.div(b, NEAR // 8), lax.rem(b, NEAR // 8) * 8
            block = pl.ds(pl.multiple_of(r0, 8), 8)
            values = [recv_a[g][j, fi, block, :] for j in range(SLOTS)]
            for n in range(SLOTS):
                total = None
                for j in range(SLOTS):
                    if j == n:
                        continue
                    term = coef[max(j, n), min(j, n)] * values[j]
                    if total is None:
                        total = term if j > n else -term
                    else:
                        total = total + term if j > n else total - term
                mixed[g][n, fi, block, :] = total

        for k in (5, 3, 7, 1, 4, 2, 6):
            send_c(g, k).start()
        own_c[g].start()

    for copy in consts:
        copy.wait()
    met(0)
    greet(1)
    for g in range(count):
        mix(g)
        if g == 0:
            met(1)
            greet(2)

    for copy in loads:
        copy.wait()
    for copy in halos[0]:
        copy.wait_recv()

    window = NEAR + 8
    shape = (window, CELLS_X)
    col = lax.broadcasted_iota(jnp.int32, shape, 1)

    def stencil(part):
        base = part * (CYCLES - window)
        span = pl.ds(base, window)
        keep = slice(8 * part, 8 * part + NEAR)
        target = pl.ds(part * NEAR, NEAR)
        row = lax.broadcasted_iota(jnp.int32, shape, 0) + base

        @pl.loop(0, SECTOR)
        def _(t):
            mu = mux[t + 1, span]
            half_cycle = 0.5 / (row[keep].astype(jnp.float32) + 1.0)
            up = half_cycle * (mu[keep] + mux[t + 2, target])
            down = half_cycle * (mu[keep] + mux[t, target])
            out_r = jnp.where(
                row < CYCLES - 1, 0.5 * (mu + pltpu.roll(mu, window - 1, 0)), 0.0
            )
            in_r = jnp.where(row > 0, pltpu.roll(out_r, 1, 0), 0.0)
            out_x = jnp.where(
                col < CELLS_X - 1, 0.5 * (mu + pltpu.roll(mu, CELLS_X - 1, 1)), 0.0
            )
            in_x = pltpu.roll(out_x, 1, 1)
            own = up + down + (out_r + in_r + out_x + in_x)[keep]
            for f in range(FIELDS):
                p = adjx[f, t + 1, span]
                face = [1.0 - bcf[i, f].astype(jnp.float32) for i in range(3)]
                edge = (
                    jnp.where(row[keep] == CYCLES - 1, face[2], 0.0)
                    + jnp.where(col[keep] == 0, face[0], 0.0)
                    + jnp.where(col[keep] == CELLS_X - 1, face[1], 0.0)
                )
                core = p[keep]
                diffused = (own + edge * mu[keep]) * core
                diffused = diffused - up * adjx[f, t + 2, target] - down * adjx[f, t, target]
                diffused = diffused - (out_r * pltpu.roll(p, window - 1, 0))[keep]
                diffused = diffused - (in_r * pltpu.roll(p, 1, 0))[keep]
                diffused = diffused - out_x[keep] * pltpu.roll(core, CELLS_X - 1, 1)
                diffused = diffused - in_x[keep] * pltpu.roll(core, 1, 1)
                total = local[f, t, target] + kap[f] * diffused
                for g in range(FIELDS):
                    total = total + cpl[g, f] * adjx[g, t + 1, target]
                local[f, t, target] = total

    stencil(0)
    met(2)
    greet(3)

    for g in range(count):
        lo, hi, _ = bounds[g]
        own_c[g].wait()
        for k in range(1, SLOTS):
            arrive_c(g, k).wait_recv()
        stride = (hi - lo) * SECTOR

        @pl.loop(0, SECTOR)
        def _(t):
            for f in range(lo, hi):
                for b in range(NEAR // 8):
                    block = pl.ds(b * 8, 8)
                    value = local[f, t, block, :] + spec[g][f - lo, t, block, :]
                    start = b * 8 * stride + (f - lo) * SECTOR + t
                    stage_e[g][pl.ds(start, 8, stride=stride), :] = value

        if g == 0:
            met(3)
        own_e[g].start()

        for i in range(1, SECTORS):
            send_s(stage_e, recv_e, e_send, e_recv, g, SECTORS - i, sp).start()

    for k in (5, 3, 7, 1, 4, 2, 6):
        send_a(count, k).start()
    for copy in halos[1]:
        copy.start()

    for g in range(count):
        lo, hi, _ = bounds[g]
        own_e[g].wait()

        for i in range(1, SECTORS):
            send_s(
                stage_e, recv_e, e_send, e_recv, g, SECTORS - i, sp
            ).wait_recv()

        pencils = recv_e[g][...].reshape(SECTORS, (hi - lo) * SECTOR, CELLS_X)
        parts = []
        for f in range(hi - lo):
            pencil = pencils[:, f * SECTOR : (f + 1) * SECTOR, :].reshape(POINTS, CELLS_X)
            smooth = jnp.dot(
                mtab[...],
                pencil,
                precision=lax.Precision.HIGHEST,
                preferred_element_type=jnp.float32,
            )
            parts.append(smooth.reshape(SECTORS, SECTOR, CELLS_X))
        stage_g[g][...] = jnp.concatenate(parts, axis=1).reshape(
            SECTORS * (hi - lo) * SECTOR, CELLS_X
        )
        own_g[g].start()

        for i in range(1, SECTORS):
            send_s(stage_g, recv_g, g_send, g_recv, g, SECTORS - i, sp).start()

    mix(count)
    for copy in halos[1]:
        copy.wait_recv()
    stencil(1)
    own_c[count].wait()
    for k in range(1, SLOTS):
        arrive_c(count, k).wait_recv()

    @pl.loop(0, SECTOR)
    def _(t):
        for f in range(FIELDS):
            out[0, f, t, pl.ds(NEAR, NEAR), :] = (
                local[f, t, pl.ds(NEAR, NEAR), :] + spec[count][f, t]
            )

    for g in range(count):
        lo, hi, _ = bounds[g]
        own_g[g].wait()

        for i in range(1, SECTORS):
            send_s(
                stage_g, recv_g, g_send, g_recv, g, SECTORS - i, sp
            ).wait_recv()

        stride = (hi - lo) * SECTOR

        @pl.loop(0, SECTOR)
        def _(t):
            for f in range(lo, hi):
                for b in range(NEAR // 8):
                    start = b * 8 * stride + (f - lo) * SECTOR + t
                    out[0, f, t, pl.ds(b * 8, 8), :] = recv_g[g][
                        pl.ds(start, 8, stride=stride), :
                    ]

    for copy in halos[0] + halos[1]:
        copy.wait_send()
    for g in range(count + 1):
        for k in range(1, SLOTS):
            send_a(g, k).wait_send()
            send_c(g, k).wait_send()
    for g in range(count):

        for i in range(1, SECTORS):
            send_s(stage_e, recv_e, e_send, e_recv, g, SECTORS - i, sp).wait_send()
            send_s(stage_g, recv_g, g_send, g_recv, g, SECTORS - i, sp).wait_send()


def body(adjoint, source, viscosity, kappa, coupling, bc_flags, inst_map):
    count = len(GROUPS)
    sizes = [hi - lo for lo, hi in GROUPS]
    f32 = jnp.float32
    vmem, dma = pltpu.VMEM, pltpu.SemaphoreType.DMA
    slabs = [vmem((SLOTS, n, NEAR, CELLS_X), f32) for n in sizes + [FIELDS]]
    sectors = [vmem((n, SECTOR, NEAR, CELLS_X), f32) for n in sizes + [FIELDS]]
    pencils = [vmem((SECTORS * n * SECTOR, CELLS_X), f32) for n in sizes]
    scratch = [
        vmem((FIELDS, SECTOR + 2, CYCLES, CELLS_X), f32),
        vmem((SECTOR + 2, CYCLES, CELLS_X), f32),
        vmem((FIELDS, SECTOR, CYCLES, CELLS_X), f32),
        vmem((POINTS, POINTS), f32),
        *slabs,
        *slabs,
        *sectors,
        *(pencils * 4),
        dma((8,)),
        dma((8,)),
        dma((8,)),
        dma((4, count + 1)),
        pltpu.SemaphoreType.REGULAR((4,)),
        *[
            pltpu.SMEM(x.shape, x.dtype)
            for x in (kappa, coupling, bc_flags.T, inst_map, slot_table())
        ],
        *[dma((count + 1, SLOTS))] * 4,
        *[dma((count, SECTORS))] * 4,
    ]
    hbm = pl.BlockSpec(memory_space=pltpu.HBM)
    return pl.pallas_call(
        kernel,
        out_shape=jax.ShapeDtypeStruct(adjoint.shape, f32),
        in_specs=[hbm] * 8,
        out_specs=pl.BlockSpec(memory_space=pltpu.VMEM),
        scratch_shapes=scratch,
        compiler_params=pltpu.CompilerParams(
            collective_id=0, has_side_effects=True, vmem_limit_bytes=48 * 1024 * 1024
        ),
        name="residual",
    )(*[
        pltpu.with_memory_space_constraint(x, pltpu.HBM)
        for x in (
            adjoint, source, viscosity, kappa, coupling, bc_flags.T, inst_map, slot_table()
        )
    ])


def solution(mesh):
    return jax.shard_map(
        body,
        mesh=mesh,
        in_specs=(
            P("inst", None, "space", None, None),
            P("inst", None, "space", None, None),
            P("space", None, None),
            P(),
            P(),
            P(),
            P(),
        ),
        out_specs=P("inst", None, "space", None, None),
        check_vma=False,
    )
```

```python
import functools

import jax
import jax.numpy as jnp
import numpy as np
from jax import lax
from jax.experimental import pallas as pl
from jax.experimental.pallas import tpu as pltpu
from jax.sharding import PartitionSpec as P

FIELDS, SECTOR, CYCLES, CELLS_X = 5, 8, 64, 128
POINTS, NEAR, SLOTS, SECTORS = 256, 32, 8, 32
GROUPS = ((0, 2), (2, 5))
MESH = pl.DeviceIdType.MESH


def slot_table():
    offset = np.arange(-(SLOTS - 1), SLOTS + 1)
    parity = 1.0 - 2.0 * (np.abs(offset) % 2)
    sines = np.sin(np.pi * offset / SLOTS)
    inner = (offset != 0) & (np.abs(offset) < SLOTS)
    table = np.where(inner, 0.5 * parity / np.where(inner, sines, 1.0), 0.0)
    return jnp.asarray(table.astype(np.float32))


def kernel(adj, src, visc, *refs):
    smalls, out, scratch = refs[:5], refs[5], refs[6:]
    count = len(GROUPS)
    names = iter(scratch)
    take = lambda n: [next(names) for _ in range(n)]
    adjx, mux, local, mtab = take(4)
    recv_a = take(count + 1)
    mixed = take(count + 1)
    spec = take(count + 1)
    stage_e, recv_e, stage_g, recv_g = take(count), take(count), take(count), take(count)
    load_sem, halo_send, halo_recv, own_sem, ready = take(5)
    mhead, mrest = take(2)
    held = take(5)
    kap, cpl, bcf, imap, tab = held
    a_send, a_recv, c_send, c_recv = take(4)
    e_send, e_recv, g_send, g_recv = take(4)

    me, sp = lax.axis_index("inst"), lax.axis_index("space")
    ix, iy = lax.div(me, 2), lax.rem(me, 2)
    sz, sy, sc = lax.div(sp, 4), lax.rem(lax.div(sp, 2), 2), lax.rem(sp, 2)

    flip_y = [iy, lax.rem(iy + 1, 2)]
    turn_x = [lax.rem(ix + k, 4) * 2 for k in range(4)]
    turn_z = [lax.rem(sz + k, 8) * 4 for k in range(8)]
    flip_s = [sy * 2, lax.rem(sy + 1, 2) * 2]
    flip_c = [sc, lax.rem(sc + 1, 2)]

    def inst_at(k, sign):
        return turn_x[(sign * (k // 2)) % 4] + flip_y[k % 2]

    def space_at(i, sign):
        step = i // 2 % 8
        kz = (step + 1) // 2 * (1 - 2 * (step % 2))
        return turn_z[(sign * kz) % 8] + flip_s[i // 16] + flip_c[i % 2]

    loads = [
        pltpu.make_async_copy(visc, mux.at[pl.ds(1, SECTOR)], load_sem.at[0]),
        pltpu.make_async_copy(adj.at[0], adjx.at[:, pl.ds(1, SECTOR)], load_sem.at[1]),
        pltpu.make_async_copy(src.at[0], local, load_sem.at[2]),
    ]
    consts = [
        pltpu.make_async_copy(small, ref, load_sem.at[3 + i])
        for i, (small, ref) in enumerate(zip(smalls, held))
    ]
    bounds = [(lo, hi, 0) for lo, hi in GROUPS] + [(0, FIELDS, NEAR)]

    def chunk(g, slot):
        lo, hi, first = bounds[g]
        return adj.at[0, pl.ds(lo, hi - lo), slot, pl.ds(first, NEAR), :]

    own_a = [
        pltpu.make_async_copy(chunk(g, me), recv_a[g].at[me], own_sem.at[0, g])
        for g in range(count + 1)
    ]
    own_c = [
        pltpu.make_async_copy(mixed[g].at[me], spec[g].at[:, me], own_sem.at[1, g])
        for g in range(count + 1)
    ]

    def rows(g, index):
        depth = (bounds[g][1] - bounds[g][0]) * SECTOR
        return pl.ds(pl.multiple_of(index * depth, 8), depth)

    own_e = [
        pltpu.make_async_copy(
            stage_e[g].at[rows(g, sp)], recv_e[g].at[rows(g, sp)], own_sem.at[2, g]
        )
        for g in range(count)
    ]
    own_g = [
        pltpu.make_async_copy(
            stage_g[g].at[rows(g, sp)], recv_g[g].at[rows(g, sp)], own_sem.at[3, g]
        )
        for g in range(count)
    ]

    def send_a(g, k):
        return pltpu.make_async_remote_copy(
            src_ref=chunk(g, inst_at(k, 1)),
            dst_ref=recv_a[g].at[me],
            send_sem=a_send.at[g, k],
            recv_sem=a_recv.at[g, k],
            device_id={"inst": inst_at(k, 1)},
            device_id_type=MESH,
        )

    def arrive_a(g, k):
        return pltpu.make_async_remote_copy(
            src_ref=chunk(g, me),
            dst_ref=recv_a[g].at[inst_at(k, -1)],
            send_sem=a_send.at[g, k],
            recv_sem=a_recv.at[g, k],
            device_id={"inst": inst_at(k, 1)},
            device_id_type=MESH,
        )

    def send_c(g, k):
        return pltpu.make_async_remote_copy(
            src_ref=mixed[g].at[inst_at(k, 1)],
            dst_ref=spec[g].at[:, me],
            send_sem=c_send.at[g, k],
            recv_sem=c_recv.at[g, k],
            device_id={"inst": inst_at(k, 1)},
            device_id_type=MESH,
        )

    def arrive_c(g, k):
        return pltpu.make_async_remote_copy(
            src_ref=mixed[g].at[me],
            dst_ref=spec[g].at[:, inst_at(k, -1)],
            send_sem=c_send.at[g, k],
            recv_sem=c_recv.at[g, k],
            device_id={"inst": inst_at(k, 1)},
            device_id_type=MESH,
        )

    def send_s(stage, recv, send_sem, recv_sem, g, i, slot):
        return pltpu.make_async_remote_copy(
            src_ref=stage[g].at[rows(g, space_at(i, 1))],
            dst_ref=recv[g].at[rows(g, slot)],
            send_sem=send_sem.at[g, i],
            recv_sem=recv_sem.at[g, i],
            device_id={"space": space_at(i, 1)},
            device_id_type=MESH,
        )

    after, before = lax.rem(sp + 1, SECTORS), lax.rem(sp + SECTORS - 1, SECTORS)

    def halo(index, source, target, peer):
        return pltpu.make_async_remote_copy(
            src_ref=source,
            dst_ref=target,
            send_sem=halo_send.at[index],
            recv_sem=halo_recv.at[index],
            device_id={"space": peer},
            device_id_type=MESH,
        )

    def halos_of(part):
        span = pl.ds(part * NEAR, NEAR)
        first, last = SECTOR - 1, SECTOR + 1
        return [
            halo(4 * part, adj.at[0, :, first, span], adjx.at[:, 0, span], after),
            halo(4 * part + 1, adj.at[0, :, 0, span], adjx.at[:, last, span], before),
            halo(4 * part + 2, visc.at[first, span], mux.at[0, span], after),
            halo(4 * part + 3, visc.at[0, span], mux.at[last, span], before),
        ]

    halos = [halos_of(0), halos_of(1)]

    barrier = pltpu.get_barrier_semaphore()
    for k in range(1, SLOTS):
        pl.semaphore_signal(
            barrier, inc=1, device_id={"inst": inst_at(k, 1)}, device_id_type=MESH
        )

    for peer in (after, before):
        pl.semaphore_signal(barrier, inc=1, device_id={"space": peer}, device_id_type=MESH)

    def greet(j):
        for sign in (1, -1):
            peer = lax.rem(sp + sign * 2**j + SECTORS, SECTORS)
            pl.semaphore_signal(
                ready.at[j], inc=1, device_id={"space": peer}, device_id_type=MESH
            )

    def met(j):
        pl.semaphore_wait(ready.at[j], 2)

    for copy in consts + loads:
        copy.start()
    for copy in own_a:
        copy.start()
    pl.semaphore_wait(barrier, SLOTS - 1 + 2)
    greet(0)

    for g in range(count):
        for k in (5, 3, 7, 1, 4, 2, 6):
            send_a(g, k).start()
    for copy in halos[0]:
        copy.start()

    cutoff = jnp.maximum(4, lax.div(POINTS * (sp + 1), 2 * NEAR))
    width = 2 * cutoff - 1
    weight = 1.0 - sp.astype(jnp.float32) / NEAR

    @pl.loop(0, POINTS // 32)
    def _(b):
        row = lax.broadcasted_iota(jnp.int32, (32, POINTS), 0) + b * 32
        col = lax.broadcasted_iota(jnp.int32, (32, POINTS), 1)
        gap = (row - col + POINTS) & (POINTS - 1)
        top = jnp.sin(((gap * width) & (2 * POINTS - 1)).astype(jnp.float32) * (np.pi / POINTS))
        low = jnp.sin(gap.astype(jnp.float32) * (np.pi / POINTS))
        same = gap == 0
        ratio = top / jnp.where(same, 1.0, low)
        table = jnp.where(same, width.astype(jnp.float32), ratio) * (1.0 / POINTS)
        mtab[pl.ds(pl.multiple_of(b * 32, 32), 32), :] = weight * table + jnp.where(
            same, 1.0 - weight, 0.0
        )

    whole = mtab[...]
    mhead[...] = whole.astype(jnp.bfloat16)
    mrest[...] = (whole - mhead[...].astype(jnp.float32)).astype(jnp.bfloat16)
    dot = functools.partial(jnp.dot, preferred_element_type=jnp.float32)

    def mix(g):
        own_a[g].wait()
        for k in range(1, SLOTS):
            arrive_a(g, k).wait_recv()
        fields = bounds[g][1] - bounds[g][0]
        coef = {
            (j, n): tab[imap[j] - imap[n] + SLOTS - 1]
            for n in range(SLOTS)
            for j in range(n + 1, SLOTS)
        }

        @pl.loop(0, fields * NEAR // 8)
        def _(b):
            fi, r0 = lax.div(b, NEAR // 8), lax.rem(b, NEAR // 8) * 8
            block = pl.ds(pl.multiple_of(r0, 8), 8)
            values = [recv_a[g][j, fi, block, :] for j in range(SLOTS)]
            for n in range(SLOTS):
                total = None
                for j in range(SLOTS):
                    if j == n:
                        continue
                    term = coef[max(j, n), min(j, n)] * values[j]
                    if total is None:
                        total = term if j > n else -term
                    else:
                        total = total + term if j > n else total - term
                mixed[g][n, fi, block, :] = total

        for k in (5, 3, 7, 1, 4, 2, 6):
            send_c(g, k).start()
        own_c[g].start()

    for copy in consts:
        copy.wait()
    met(0)
    greet(1)
    for g in range(count):
        mix(g)
        if g == 0:
            met(1)
            greet(2)

    for copy in loads:
        copy.wait()
    for copy in halos[0]:
        copy.wait_recv()

    window = NEAR + 8
    shape = (window, CELLS_X)
    col = lax.broadcasted_iota(jnp.int32, shape, 1)

    def stencil(part):
        base = part * (CYCLES - window)
        span = pl.ds(base, window)
        keep = slice(8 * part, 8 * part + NEAR)
        target = pl.ds(part * NEAR, NEAR)
        row = lax.broadcasted_iota(jnp.int32, shape, 0) + base

        @pl.loop(0, SECTOR)
        def _(t):
            mu = mux[t + 1, span]
            half_cycle = 0.5 / (row[keep].astype(jnp.float32) + 1.0)
            up = half_cycle * (mu[keep] + mux[t + 2, target])
            down = half_cycle * (mu[keep] + mux[t, target])
            out_r = jnp.where(
                row < CYCLES - 1, 0.5 * (mu + pltpu.roll(mu, window - 1, 0)), 0.0
            )
            in_r = jnp.where(row > 0, pltpu.roll(out_r, 1, 0), 0.0)
            out_x = jnp.where(
                col < CELLS_X - 1, 0.5 * (mu + pltpu.roll(mu, CELLS_X - 1, 1)), 0.0
            )
            in_x = pltpu.roll(out_x, 1, 1)
            own = up + down + (out_r + in_r + out_x + in_x)[keep]
            for f in range(FIELDS):
                p = adjx[f, t + 1, span]
                face = [1.0 - bcf[i, f].astype(jnp.float32) for i in range(3)]
                edge = (
                    jnp.where(row[keep] == CYCLES - 1, face[2], 0.0)
                    + jnp.where(col[keep] == 0, face[0], 0.0)
                    + jnp.where(col[keep] == CELLS_X - 1, face[1], 0.0)
                )
                core = p[keep]
                diffused = (own + edge * mu[keep]) * core
                diffused = diffused - up * adjx[f, t + 2, target] - down * adjx[f, t, target]
                diffused = diffused - (out_r * pltpu.roll(p, window - 1, 0))[keep]
                diffused = diffused - (in_r * pltpu.roll(p, 1, 0))[keep]
                diffused = diffused - out_x[keep] * pltpu.roll(core, CELLS_X - 1, 1)
                diffused = diffused - in_x[keep] * pltpu.roll(core, 1, 1)
                total = local[f, t, target] + kap[f] * diffused
                for g in range(FIELDS):
                    total = total + cpl[g, f] * adjx[g, t + 1, target]
                local[f, t, target] = total

    for k in (4, 2, 6):
        send_a(count, k).start()
    stencil(0)
    met(2)
    greet(3)

    for g in range(count):
        lo, hi, _ = bounds[g]
        own_c[g].wait()
        for k in range(1, SLOTS):
            arrive_c(g, k).wait_recv()
        stride = (hi - lo) * SECTOR

        @pl.loop(0, SECTOR)
        def _(t):
            for f in range(lo, hi):
                for b in range(NEAR // 8):
                    block = pl.ds(b * 8, 8)
                    value = local[f, t, block, :] + spec[g][f - lo, t, block, :]
                    start = b * 8 * stride + (f - lo) * SECTOR + t
                    stage_e[g][pl.ds(start, 8, stride=stride), :] = value

        if g == 0:
            met(3)
        own_e[g].start()

        for i in range(1, SECTORS):
            send_s(stage_e, recv_e, e_send, e_recv, g, SECTORS - i, sp).start()

    for k in (5, 3, 7, 1):
        send_a(count, k).start()
    for copy in halos[1]:
        copy.start()

    for g in range(count):
        lo, hi, _ = bounds[g]
        own_e[g].wait()

        for i in range(1, SECTORS):
            send_s(
                stage_e, recv_e, e_send, e_recv, g, SECTORS - i, sp
            ).wait_recv()

        pencils = recv_e[g][...].reshape(SECTORS, (hi - lo) * SECTOR, CELLS_X)
        parts = []
        for f in range(hi - lo):
            pencil = pencils[:, f * SECTOR : (f + 1) * SECTOR, :].reshape(POINTS, CELLS_X)
            head = pencil.astype(jnp.bfloat16)
            rest = (pencil - head.astype(jnp.float32)).astype(jnp.bfloat16)
            smooth = dot(mhead[...], rest) + dot(mrest[...], head) + dot(mhead[...], head)
            parts.append(smooth.reshape(SECTORS, SECTOR, CELLS_X))
        stage_g[g][...] = jnp.concatenate(parts, axis=1).reshape(
            SECTORS * (hi - lo) * SECTOR, CELLS_X
        )
        own_g[g].start()

        for i in range(1, SECTORS):
            send_s(stage_g, recv_g, g_send, g_recv, g, SECTORS - i, sp).start()

    mix(count)
    for copy in halos[1]:
        copy.wait_recv()
    stencil(1)
    own_c[count].wait()
    for k in range(1, SLOTS):
        arrive_c(count, k).wait_recv()

    @pl.loop(0, SECTOR)
    def _(t):
        for f in range(FIELDS):
            out[0, f, t, pl.ds(NEAR, NEAR), :] = (
                local[f, t, pl.ds(NEAR, NEAR), :] + spec[count][f, t]
            )

    for g in range(count):
        lo, hi, _ = bounds[g]
        own_g[g].wait()

        for i in range(1, SECTORS):
            send_s(
                stage_g, recv_g, g_send, g_recv, g, SECTORS - i, sp
            ).wait_recv()

        stride = (hi - lo) * SECTOR

        @pl.loop(0, SECTOR)
        def _(t):
            for f in range(lo, hi):
                for b in range(NEAR // 8):
                    start = b * 8 * stride + (f - lo) * SECTOR + t
                    out[0, f, t, pl.ds(b * 8, 8), :] = recv_g[g][
                        pl.ds(start, 8, stride=stride), :
                    ]

    for copy in halos[0] + halos[1]:
        copy.wait_send()
    for g in range(count + 1):
        for k in range(1, SLOTS):
            send_a(g, k).wait_send()
            send_c(g, k).wait_send()
    for g in range(count):

        for i in range(1, SECTORS):
            send_s(stage_e, recv_e, e_send, e_recv, g, SECTORS - i, sp).wait_send()
            send_s(stage_g, recv_g, g_send, g_recv, g, SECTORS - i, sp).wait_send()


def body(adjoint, source, viscosity, kappa, coupling, bc_flags, inst_map):
    count = len(GROUPS)
    sizes = [hi - lo for lo, hi in GROUPS]
    f32 = jnp.float32
    vmem, dma = pltpu.VMEM, pltpu.SemaphoreType.DMA
    slabs = [vmem((SLOTS, n, NEAR, CELLS_X), f32) for n in sizes + [FIELDS]]
    sectors = [vmem((n, SECTOR, NEAR, CELLS_X), f32) for n in sizes + [FIELDS]]
    pencils = [vmem((SECTORS * n * SECTOR, CELLS_X), f32) for n in sizes]
    scratch = [
        vmem((FIELDS, SECTOR + 2, CYCLES, CELLS_X), f32),
        vmem((SECTOR + 2, CYCLES, CELLS_X), f32),
        vmem((FIELDS, SECTOR, CYCLES, CELLS_X), f32),
        vmem((POINTS, POINTS), f32),
        *slabs,
        *slabs,
        *sectors,
        *(pencils * 4),
        dma((8,)),
        dma((8,)),
        dma((8,)),
        dma((4, count + 1)),
        pltpu.SemaphoreType.REGULAR((4,)),
        vmem((POINTS, POINTS), jnp.bfloat16),
        vmem((POINTS, POINTS), jnp.bfloat16),
        *[
            pltpu.SMEM(x.shape, x.dtype)
            for x in (kappa, coupling, bc_flags.T, inst_map, slot_table())
        ],
        *[dma((count + 1, SLOTS))] * 4,
        *[dma((count, SECTORS))] * 4,
    ]
    hbm = pl.BlockSpec(memory_space=pltpu.HBM)
    return pl.pallas_call(
        kernel,
        out_shape=jax.ShapeDtypeStruct(adjoint.shape, f32),
        in_specs=[hbm] * 8,
        out_specs=pl.BlockSpec(memory_space=pltpu.VMEM),
        scratch_shapes=scratch,
        compiler_params=pltpu.CompilerParams(
            collective_id=0, has_side_effects=True, vmem_limit_bytes=48 * 1024 * 1024
        ),
        name="residual",
    )(*[
        pltpu.with_memory_space_constraint(x, pltpu.HBM)
        for x in (
            adjoint, source, viscosity, kappa, coupling, bc_flags.T, inst_map, slot_table()
        )
    ])


def solution(mesh):
    return jax.shard_map(
        body,
        mesh=mesh,
        in_specs=(
            P("inst", None, "space", None, None),
            P("inst", None, "space", None, None),
            P("space", None, None),
            P(),
            P(),
            P(),
            P(),
        ),
        out_specs=P("inst", None, "space", None, None),
        check_vma=False,
    )
```
